512 devices in a mesh: lat: 32 (over x_hi, y, core), lon: 16 (over z, x_lo).
Axes of the slice: x: 4 (x_hi: 2, x_lo: 2; x = x_hi * 2 + x_lo), y: 8, z: 8, core: 2. Of those that a mesh axis runs over, the one named last changes fastest.
Arguments:
- features: bfloat16 [512, 1024, 128], P('lat', 'lon'), may hold values from -6 to 6
- w_first: bfloat16 [2, 1, 128, 128], replicated, may hold values from -0.375 to 0.375
- bias_first: float32 [2, 1, 128], replicated, may hold values from -3 to 3
- w_second: bfloat16 [2, 1, 128, 128], replicated, may hold values from -0.375 to 0.375
- bias_second: float32 [2, 1, 128], replicated, may hold values from -0.3 to 0.3
Outputs:
- mixed_field: bfloat16 [512, 1024, 128], P('lat', 'lon')
The draws below stay inside these ranges and needn't reach their ends.
All inputs are finite; a program needn't handle non-finite values.
Results may differ from the reference program's by a relative error of at most 0.025.
Values may be sent and summed in bfloat16 or wider, within the bound.
A program may use at most 64 MiB of HBM per device.

```python
import math
import jax
import jax.numpy as jnp
from jax import lax

NLAT = 512
NLON = 1024
BLOCK = 128
NBLK = 1
C = 128
N_LON = 16


def block_levels(rng, shape, pieces, least, top_value):
    def one(position, shards_of):
        steps = jax.random.uniform(jax.random.fold_in(jax.random.fold_in(rng, 6), position), (shards_of,), jnp.float32, least / len(pieces), top_value / len(pieces))
        return jnp.repeat(jnp.exp(steps), shape[position] // shards_of).reshape((-1,) + (1,) * (len(shape) - position - 1))

    level = one(*pieces[0])
    for cut in pieces[1:]:
        level = level * one(*cut)
    return level


def scatter_about(stream_key, shape, deviation, most, pieces=(), held_as=jnp.bfloat16):
    entries = jax.random.normal(stream_key, shape, jnp.float32) * deviation
    if len(pieces) > 0:
        entries = block_levels(stream_key, shape, pieces, -0.22, 0.18) * entries
    return jnp.clip(entries, min=-most, max=most).astype(held_as)


def setup_inputs(seed: int = 0) -> dict:
    seeds = jax.random.split(jax.random.key(seed), 6)
    features = scatter_about(seeds[0], (NLAT, NLON, C), 1.0, 6.0, ((0, 32), (1, 16)))
    w_first = scatter_about(seeds[1], (2, NBLK, BLOCK, BLOCK), (2 * BLOCK) ** -0.5, 0.375)
    bias_first = scatter_about(seeds[2], (2, NBLK, BLOCK), 0.5, 3.0, (), jnp.float32)
    w_second = scatter_about(seeds[3], (2, NBLK, BLOCK, BLOCK), (2 * BLOCK) ** -0.5, 0.375)
    bias_second = scatter_about(seeds[4], (2, NBLK, BLOCK), 0.05, 0.3, (), jnp.float32)
    return {"features": features, "w_first": w_first, "bias_first": bias_first, "w_second": w_second, "bias_second": bias_second}


shrink_level = 0.01

def to_half(values):
    rounded = values.astype(jnp.bfloat16)
    rounded = lax.optimization_barrier(rounded)
    return rounded.astype(jnp.float32)

def round_complex(values):
    return lax.complex(to_half(jnp.real(values)), to_half(jnp.imag(values)))

def phase_parts(product, length, sign):
    angle_value = (product % length).astype(jnp.float32) * (sign * 2.0 * math.pi / length)
    return (jnp.cos(angle_value), jnp.sin(angle_value))

def phase_factor(product, length, sign):
    cos_part, sin_part = phase_parts(product, length, sign)
    return lax.complex(cos_part, sin_part)

def bit_reverse(number, levels):
    result = jnp.zeros_like(number)
    for bit_level in range(levels):
        result = result + number // 2 ** bit_level % 2 * 2 ** (levels - 1 - bit_level)
    return result

def block_sections(values, levels):
    real_part = values
    imag_part = jnp.zeros_like(values)
    full_shape = values.shape
    for section_level in range(levels - 1, -1, -1):
        half_span = 2 ** section_level
        split_shape = (full_shape[0], full_shape[1] // (2 * half_span), 2, half_span) + full_shape[2:]
        real_split = real_part.reshape(split_shape)
        imag_split = imag_part.reshape(split_shape)
        tw_cos, tw_sin = phase_parts(jnp.arange(half_span, dtype=jnp.int32), 2 * half_span, -1.0)
        tw_cos = tw_cos[None, None, :, None, None]
        tw_sin = tw_sin[None, None, :, None, None]
        sum_re = real_split[:, :, 0] + real_split[:, :, 1]
        sum_im = imag_split[:, :, 0] + imag_split[:, :, 1]
        diff_re = real_split[:, :, 0] - real_split[:, :, 1]
        diff_im = imag_split[:, :, 0] - imag_split[:, :, 1]
        upper_re = diff_re * tw_cos - diff_im * tw_sin
        upper_im = diff_re * tw_sin + diff_im * tw_cos
        real_part = to_half(jnp.stack([sum_re, upper_re], axis=2).reshape(full_shape))
        imag_part = to_half(jnp.stack([sum_im, upper_im], axis=2).reshape(full_shape))
    return (real_part, imag_part)

def block_product(real_part, imag_part, weights):
    real_out = jnp.einsum('tnj,njk->tnk', real_part, weights[0]) - jnp.einsum('tnj,njk->tnk', imag_part, weights[1])
    imag_out = jnp.einsum('tnj,njk->tnk', imag_part, weights[0]) + jnp.einsum('tnj,njk->tnk', real_part, weights[1])
    return (real_out, imag_out)

def soft_shrink(values):
    return jnp.sign(values) * jnp.maximum(jnp.abs(values) - shrink_level, 0.0)

def spectral_mix(real_part, imag_part, first_w, first_bias, second_w, second_bias):
    shape_in = real_part.shape
    blocks = first_w.shape[1]
    block_width = first_w.shape[2]
    flat_re = real_part.astype(jnp.float32).reshape(-1, blocks, block_width)
    flat_im = imag_part.astype(jnp.float32).reshape(-1, blocks, block_width)
    hid_re, hid_im = block_product(flat_re, flat_im, first_w)
    act_re = to_half(jax.nn.relu(hid_re + first_bias[0]))
    act_im = to_half(jax.nn.relu(hid_im + first_bias[1]))
    out_re, out_im = block_product(act_re, act_im, second_w)
    return (soft_shrink(out_re + second_bias[0]).astype(jnp.bfloat16).reshape(shape_in), soft_shrink(out_im + second_bias[1]).astype(jnp.bfloat16).reshape(shape_in))

def forward_group(group):
    lat_cells, total_lon, group_width = group.shape
    shard_cells = total_lon // N_LON
    keep_cells = shard_cells // 2
    levels = N_LON.bit_length() - 1
    blocks = group.astype(jnp.float32).reshape(lat_cells, N_LON, shard_cells, group_width)
    sectioned_re, sectioned_im = block_sections(blocks, levels)
    order = bit_reverse(jnp.arange(N_LON, dtype=jnp.int32), levels)
    natural = lax.complex(jnp.take(sectioned_re, order, axis=1), jnp.take(sectioned_im, order, axis=1))
    product = jnp.arange(N_LON, dtype=jnp.int32)[:, None] * jnp.arange(shard_cells, dtype=jnp.int32)[None, :]
    first_pass = round_complex(natural * phase_factor(product, total_lon, -1.0)[None, :, :, None])
    lon_spectrum = round_complex(jnp.fft.fft(first_pass, axis=2)[:, :, :keep_cells])
    spectrum = round_complex(jnp.fft.fft(lon_spectrum, axis=0) / math.sqrt(lat_cells * total_lon))
    return (jnp.real(spectrum).astype(jnp.bfloat16), jnp.imag(spectrum).astype(jnp.bfloat16))

def inverse_group(pair):
    real_part, imag_part = pair
    lat_cells, shard_count, keep_cells, group_width = real_part.shape
    shard_cells = 2 * keep_cells
    total_lon = shard_count * shard_cells
    mixed = lax.complex(real_part.astype(jnp.float32), imag_part.astype(jnp.float32))
    lat_back = round_complex(jnp.fft.ifft(mixed, axis=0) * lat_cells)
    first_row = jnp.arange(shard_count, dtype=jnp.int32)[:, None] == 0
    first_col = jnp.arange(keep_cells, dtype=jnp.int32)[None, :] == 0
    weight = jnp.where(first_row & first_col, 1.0, 2.0).astype(jnp.float32)
    weighted = lat_back * weight[None, :, :, None]
    padded = jnp.pad(weighted, ((0, 0), (0, 0), (0, shard_cells - keep_cells), (0, 0)))
    over_q = jnp.fft.ifft(padded, axis=2) * shard_cells
    product = jnp.arange(shard_count, dtype=jnp.int32)[:, None] * jnp.arange(shard_cells, dtype=jnp.int32)[None, :]
    lon_back = round_complex(over_q * phase_factor(product, total_lon, 1.0)[None, :, :, None])
    over_p = jnp.fft.ifft(lon_back, axis=1) * shard_count
    filtered = jnp.real(over_p) / math.sqrt(lat_cells * total_lon)
    return filtered.astype(jnp.bfloat16).reshape(lat_cells, total_lon, group_width)

def reference(features, w_first, bias_first, w_second, bias_second):
    lat_cells, total_lon, channels = features.shape
    group_width = math.gcd(channels, 32)
    group_count = channels // group_width
    shard_cells = total_lon // N_LON
    keep_cells = shard_cells // 2
    stacked = jnp.moveaxis(features.reshape(lat_cells, total_lon, group_count, group_width), 2, 0)
    spec_re, spec_im = lax.map(forward_group, stacked)

    def regroup(parts):
        return jnp.moveaxis(parts, 0, 3).reshape(lat_cells, N_LON, keep_cells, channels)
    spec_re = regroup(spec_re)
    spec_im = regroup(spec_im)
    first_w = w_first.astype(jnp.float32)
    second_w = w_second.astype(jnp.float32)
    first_bias = bias_first.astype(jnp.float32)
    second_bias = bias_second.astype(jnp.float32)

    def mix_row(pair):
        return spectral_mix(pair[0], pair[1], first_w, first_bias, second_w, second_bias)
    mix_re, mix_im = lax.map(mix_row, (spec_re, spec_im))

    def split_groups(parts):
        return jnp.moveaxis(parts.reshape(lat_cells, N_LON, keep_cells, group_count, group_width), 3, 0)
    filtered = lax.map(inverse_group, (split_groups(mix_re), split_groups(mix_im)))
    filtered = jnp.moveaxis(filtered, 0, 2).reshape(lat_cells, total_lon, channels)
    return (features.astype(jnp.float32) + filtered.astype(jnp.float32)).astype(jnp.bfloat16)
```

```python
import functools
import math

import jax
import jax.numpy as jnp
import numpy as np
from jax import lax
from jax.experimental import pallas as pl
from jax.experimental.pallas import tpu as pltpu
from jax.sharding import PartitionSpec as P

shrink_level = 0.01
MESH = pl.DeviceIdType.MESH


def tables(total_lat, total_lon):
    waves = total_lon // 2
    turn = np.outer(np.arange(waves), np.arange(total_lon)) % total_lon
    angle = turn * (2.0 * math.pi / total_lon)
    lon_cos, lon_sin = np.cos(angle), np.sin(angle)
    lon_forward = np.stack([lon_cos, -lon_sin], axis=1).reshape(2 * waves, total_lon)
    weight = np.where(np.arange(waves) == 0, 1.0, 2.0)[:, None]
    lon_inverse = np.stack([weight * lon_cos, -weight * lon_sin], axis=1)
    lon_inverse = lon_inverse.reshape(2 * waves, total_lon).T
    turn = np.outer(np.arange(total_lat), np.arange(total_lat)) % total_lat
    angle = turn * (2.0 * math.pi / total_lat)
    lat_cos, lat_sin = np.cos(angle), np.sin(angle)
    lat_forward = np.zeros((2, total_lat, total_lat, 2))
    lat_forward[0, :, :, 0] = lat_cos
    lat_forward[0, :, :, 1] = lat_sin
    lat_forward[1, :, :, 0] = -lat_sin
    lat_forward[1, :, :, 1] = lat_cos
    lat_forward = lat_forward.reshape(2 * total_lat, 2 * total_lat)
    lat_inverse = lat_forward.T
    return [
        np.ascontiguousarray(t).astype(jnp.bfloat16)
        for t in (lon_forward, lat_forward, lat_inverse, lon_inverse)
    ]


def mixer_kernel(
    lat_count,
    lon_count,
    x_ref,
    t1_hbm,
    t2_hbm,
    t3_hbm,
    t4_hbm,
    w1_ref,
    b1_ref,
    w2_ref,
    b2_ref,
    out_ref,
    t1,
    t2,
    t3,
    t4,
    line,
    spec,
    part,
    column,
    mixed,
    back,
    rows,
    waves,
    field,
    send_sem,
    recv_sem,
    table_sem,
):
    lat = lax.axis_index("lat")
    lon = lax.axis_index("lon")
    cells = x_ref.shape[1]
    norm = 1.0 / math.sqrt(lat_count * x_ref.shape[0] * lon_count * cells)

    table_copies = [
        pltpu.make_async_copy(hbm, vmem, table_sem.at[n])
        for n, (hbm, vmem) in enumerate(((t1_hbm, t1), (t2_hbm, t2), (t3_hbm, t3), (t4_hbm, t4)))
    ]
    for copy in table_copies:
        copy.start()

    barrier = pltpu.get_barrier_semaphore()

    def greet_lon(step, _):
        peer = lax.rem(lon + step, lon_count)
        pl.semaphore_signal(barrier, inc=1, device_id={"lon": peer}, device_id_type=MESH)
        return 0

    def greet_lat(step, _):
        peer = lax.rem(lat + step, lat_count)
        pl.semaphore_signal(barrier, inc=1, device_id={"lat": peer}, device_id_type=MESH)
        return 0

    lax.fori_loop(1, lon_count, greet_lon, 0)
    lax.fori_loop(1, lat_count, greet_lat, 0)
    pl.semaphore_wait(barrier, lon_count + lat_count - 2)

    def exchange(stage, axis, me, count, source, target):
        own = pltpu.make_async_copy(source(me), target, recv_sem.at[stage])
        own.start()

        def send(step, _):
            peer = lax.rem(me + step, count)
            pltpu.make_async_remote_copy(
                src_ref=source(peer),
                dst_ref=target,
                send_sem=send_sem.at[stage],
                recv_sem=recv_sem.at[stage],
                device_id={axis: peer},
                device_id_type=MESH,
            ).start()
            return 0

        lax.fori_loop(1, count, send, 0)

    def arrived(stage, landing):
        pltpu.make_async_copy(landing, landing, recv_sem.at[stage]).wait()

    def aligned(index, size):
        return pl.ds(pl.multiple_of(index * size, size), size)

    exchange(0, "lon", lon, lon_count, lambda p: x_ref.at[p], line.at[aligned(lon, cells)])
    table_copies[0].wait()
    arrived(0, line)
    spec[...] = jnp.dot(t1[...], line[...], preferred_element_type=jnp.float32).astype(spec.dtype)

    exchange(1, "lon", lon, lon_count, lambda p: spec.at[aligned(p, cells)], part.at[lon])
    arrived(1, part)

    exchange(2, "lat", lat, lat_count, lambda p: part.at[:, aligned(p, 2)], column.at[lat])
    table_copies[1].wait()
    arrived(2, column)
    height = t2.shape[0] // 2
    spectrum = jnp.dot(
        t2[...], column.reshape(2 * height, 128)[...], preferred_element_type=jnp.float32
    )
    spectrum = (spectrum * norm).astype(jnp.bfloat16)

    def product(left_re, left_im, w_ref):
        w_re, w_im = w_ref[0, 0], w_ref[1, 0]
        re = jnp.dot(left_re, w_re, preferred_element_type=jnp.float32) - jnp.dot(
            left_im, w_im, preferred_element_type=jnp.float32
        )
        im = jnp.dot(left_im, w_re, preferred_element_type=jnp.float32) + jnp.dot(
            left_re, w_im, preferred_element_type=jnp.float32
        )
        return re, im

    def shrink(v):
        return jnp.maximum(v - shrink_level, 0.0) + jnp.minimum(v + shrink_level, 0.0)

    hid_re, hid_im = product(spectrum[:height], spectrum[height:], w1_ref)
    act_re = jnp.maximum(hid_re + b1_ref[0], 0.0).astype(jnp.bfloat16)
    act_im = jnp.maximum(hid_im + b1_ref[1], 0.0).astype(jnp.bfloat16)
    out_re, out_im = product(act_re, act_im, w2_ref)
    mixed[:height] = shrink(out_re + b2_ref[0]).astype(jnp.bfloat16)
    mixed[height:] = shrink(out_im + b2_ref[1]).astype(jnp.bfloat16)
    table_copies[2].wait()
    back[...] = jnp.dot(t3[...], mixed[...], preferred_element_type=jnp.float32).astype(back.dtype)

    exchange(3, "lat", lat, lat_count, lambda p: back.at[aligned(p, 32)], rows.at[lat])
    arrived(3, rows)

    exchange(4, "lon", lon, lon_count, lambda p: rows.at[:, aligned(p, 2)], waves.at[lon])
    table_copies[3].wait()
    arrived(4, waves)
    filtered = jnp.dot(
        t4[...], waves.reshape(t4.shape[1], 128)[...], preferred_element_type=jnp.float32
    )
    field[...] = (filtered * norm).astype(field.dtype)

    exchange(5, "lon", lon, lon_count, lambda p: field.at[aligned(p, cells)], out_ref.at[lon])
    arrived(5, out_ref)

    for stage, (buffer, count) in enumerate(
        ((line, lon_count), (line, lon_count), (line, lat_count), (line, lat_count), (line, lon_count), (line, lon_count))
    ):
        sent = line.shape[0] // count * (count - 1)
        left = line.at[pl.ds(0, sent)]
        pltpu.make_async_copy(left, left, send_sem.at[stage]).wait()


def body(mesh, features, w_first, bias_first, w_second, bias_second):
    lat_rows, lon_cells, channels = features.shape
    lat_count, lon_count = mesh.shape["lat"], mesh.shape["lon"]
    total_lat, total_lon = lat_rows * lat_count, lon_cells * lon_count
    consts = [jnp.asarray(t) for t in tables(total_lat, total_lon)]
    any_space = pl.BlockSpec(memory_space=pl.ANY)
    vmem = pl.BlockSpec(memory_space=pltpu.VMEM)
    half = jnp.bfloat16
    waves_own = total_lon // 2 // lon_count
    flat = pltpu.VMEM((total_lon, channels), half)
    filtered = pl.pallas_call(
        functools.partial(mixer_kernel, lat_count, lon_count),
        out_shape=jax.ShapeDtypeStruct((lat_rows, lon_cells, channels), half),
        in_specs=[any_space] * 5 + [vmem] * 4,
        out_specs=any_space,
        scratch_shapes=[pltpu.VMEM(t.shape, half) for t in consts]
        + [
            flat,
            flat,
            pltpu.VMEM((lon_count, 2 * waves_own, channels), half),
            pltpu.VMEM((lat_count, lat_rows, 2, channels), half),
            pltpu.VMEM((2 * total_lat, channels), half),
            pltpu.VMEM((2 * total_lat, channels), half),
            pltpu.VMEM((lat_count, 2 * lat_rows, channels), half),
            pltpu.VMEM((lon_count, waves_own, 2, channels), half),
            flat,
            pltpu.SemaphoreType.DMA((6,)),
            pltpu.SemaphoreType.DMA((6,)),
            pltpu.SemaphoreType.DMA((4,)),
        ],
        compiler_params=pltpu.CompilerParams(
            collective_id=0, has_side_effects=True, vmem_limit_bytes=48 * 2**20
        ),
    )(features, *consts, w_first, bias_first, w_second, bias_second)
    return (features.astype(jnp.float32) + filtered.astype(jnp.float32)).astype(features.dtype)


def solution(mesh):
    in_specs = (P("lat", "lon", None), P(), P(), P(), P())
    out_specs = P("lat", "lon", None)
    return jax.shard_map(
        functools.partial(body, mesh),
        mesh=mesh,
        in_specs=in_specs,
        out_specs=out_specs,
        check_vma=False,
    )
```

```python
import functools
import math

import jax
import jax.numpy as jnp
import numpy as np
from jax import lax
from jax.experimental import pallas as pl
from jax.experimental.pallas import tpu as pltpu
from jax.sharding import PartitionSpec as P

shrink_level = 0.01
MESH = pl.DeviceIdType.MESH


def wave(turn, length):
    angle = (turn % length) * (2.0 * math.pi / length)
    return np.cos(angle), np.sin(angle)


def table_bases(total_lat, total_lon):
    waves = np.arange(total_lon // 2)
    cells = np.arange(total_lon)
    lats = np.arange(total_lat)
    group = np.arange(32)
    fine = np.arange(16)
    out = []
    c, s = wave(16 * np.outer(group, cells), total_lon)
    pc, ps = wave(np.outer(fine, cells), total_lon)
    p = np.stack([pc, -ps], axis=1).reshape(32, -1)
    q = np.stack([-ps, -pc], axis=1).reshape(32, -1)
    out.append((c, s, p, q))
    c, s = wave(16 * np.outer(group, np.repeat(lats, 2)), total_lat)
    pc, ps = wave(np.outer(fine, lats), total_lat)
    p = np.stack([np.stack([pc, ps], 2), np.stack([-ps, pc], 2)]).reshape(32, -1)
    q = np.stack([np.stack([-ps, pc], 2), np.stack([-pc, -ps], 2)]).reshape(32, -1)
    out.append((c, s, p, q))
    c, s = wave(16 * np.outer(group, np.tile(lats, 2)), total_lat)
    pc, ps = wave(np.outer(fine, lats), total_lat)
    p = np.stack([np.stack([pc, -ps], 1), np.stack([ps, pc], 1)], 1).reshape(32, -1)
    q = np.stack([np.stack([-ps, -pc], 1), np.stack([pc, -ps], 1)], 1).reshape(32, -1)
    out.append((c, s, p, q))
    c, s = wave(32 * np.outer(group, np.repeat(waves, 2)), total_lon)
    pc, ps = wave(np.outer(group, waves), total_lon)
    p = np.stack([pc, -ps], axis=2).reshape(32, -1)
    q = np.stack([-ps, -pc], axis=2).reshape(32, -1)
    out.append((c, s, p, q))
    return np.stack([np.stack(kind) for kind in out]).astype(np.float32)


def mixer_kernel(
    lat_count,
    lon_count,
    x_ref,
    bases_hbm,
    w1_hbm,
    b1_hbm,
    w2_hbm,
    b2_hbm,
    out_ref,
    bases,
    w1_ref,
    b1_ref,
    w2_ref,
    b2_ref,
    t1,
    t2,
    t3,
    t4,
    line,
    spec,
    part,
    column,
    mixed,
    back,
    rows,
    waves,
    field,
    send_sem,
    recv_sem,
    table_sem,
):
    lat = lax.axis_index("lat")
    lon = lax.axis_index("lon")
    cells = x_ref.shape[1]
    norm = 1.0 / math.sqrt(lat_count * x_ref.shape[0] * lon_count * cells)

    def aligned(index, size):
        return pl.ds(pl.multiple_of(index * size, size), size)

    fetches = [
        pltpu.make_async_copy(bases_hbm.at[n], bases.at[n], table_sem.at[n]) for n in range(4)
    ] + [
        pltpu.make_async_copy(hbm, vmem, table_sem.at[4 + n])
        for n, (hbm, vmem) in enumerate(
            ((w1_hbm, w1_ref), (b1_hbm, b1_ref), (w2_hbm, w2_ref), (b2_hbm, b2_ref))
        )
    ]
    for copy in fetches:
        copy.start()

    def build(n, table):
        fetches[n].wait()

        def group(g, _):
            c = bases[n, 0, pl.ds(g, 1), :]
            s = bases[n, 1, pl.ds(g, 1), :]
            if n == 1:
                for part in range(2):
                    near = pl.ds(16 * part, 16)
                    block = c * bases[n, 2, near, :] + s * bases[n, 3, near, :]
                    first = pl.multiple_of(table.shape[0] // 2 * part + 16 * g, 16)
                    table[pl.ds(first, 16), :] = block.astype(table.dtype)
            else:
                block = c * bases[n, 2] + s * bases[n, 3]
                table[aligned(g, 32), :] = block.astype(table.dtype)
            return 0

        lax.fori_loop(0, 32, group, 0)

    barrier = pltpu.get_barrier_semaphore()

    def greet_lon(step, _):
        peer = lax.rem(lon + step, lon_count)
        pl.semaphore_signal(barrier, inc=1, device_id={"lon": peer}, device_id_type=MESH)
        return 0

    def greet_lat(step, _):
        peer = lax.rem(lat + step, lat_count)
        pl.semaphore_signal(barrier, inc=1, device_id={"lat": peer}, device_id_type=MESH)
        return 0

    lax.fori_loop(1, lon_count, greet_lon, 0)
    lax.fori_loop(1, lat_count, greet_lat, 0)
    pl.semaphore_wait(barrier, lon_count + lat_count - 2)

    def exchange(stage, axis, me, count, source, target):
        own = pltpu.make_async_copy(source(me), target, recv_sem.at[stage])
        own.start()

        def send(step, _):
            peer = lax.rem(me + step, count)
            pltpu.make_async_remote_copy(
                src_ref=source(peer),
                dst_ref=target,
                send_sem=send_sem.at[stage],
                recv_sem=recv_sem.at[stage],
                device_id={axis: peer},
                device_id_type=MESH,
            ).start()
            return 0

        lax.fori_loop(1, count, send, 0)

    def arrived(stage, landing):
        pltpu.make_async_copy(landing, landing, recv_sem.at[stage]).wait()

    exchange(0, "lon", lon, lon_count, lambda p: x_ref.at[p], line.at[aligned(lon, cells)])
    build(0, t1)
    arrived(0, line)
    spec[...] = jnp.dot(t1[...], line[...], preferred_element_type=jnp.float32).astype(spec.dtype)

    exchange(1, "lon", lon, lon_count, lambda p: spec.at[aligned(p, cells)], part.at[lon])
    build(1, t2)
    arrived(1, part)

    exchange(2, "lat", lat, lat_count, lambda p: part.at[:, aligned(p, 2)], column.at[lat])
    build(2, t3)
    for copy in fetches[4:]:
        copy.wait()
    arrived(2, column)
    height = t2.shape[0] // 2
    spectrum = jnp.dot(
        t2[...], column.reshape(2 * height, 128)[...], preferred_element_type=jnp.float32
    )
    spectrum = (spectrum * norm).astype(jnp.bfloat16)

    def product(left_re, left_im, w_ref):
        w_re, w_im = w_ref[0, 0], w_ref[1, 0]
        re = jnp.dot(left_re, w_re, preferred_element_type=jnp.float32) - jnp.dot(
            left_im, w_im, preferred_element_type=jnp.float32
        )
        im = jnp.dot(left_im, w_re, preferred_element_type=jnp.float32) + jnp.dot(
            left_re, w_im, preferred_element_type=jnp.float32
        )
        return re, im

    def shrink(v):
        return jnp.maximum(v - shrink_level, 0.0) + jnp.minimum(v + shrink_level, 0.0)

    hid_re, hid_im = product(spectrum[:height], spectrum[height:], w1_ref)
    act_re = jnp.maximum(hid_re + b1_ref[0], 0.0).astype(jnp.bfloat16)
    act_im = jnp.maximum(hid_im + b1_ref[1], 0.0).astype(jnp.bfloat16)
    out_re, out_im = product(act_re, act_im, w2_ref)
    weight = jnp.where(lat + lon == 0, 0.5, 1.0)
    mixed[:height] = (shrink(out_re + b2_ref[0]) * weight).astype(jnp.bfloat16)
    mixed[height:] = (shrink(out_im + b2_ref[1]) * weight).astype(jnp.bfloat16)
    back[...] = jnp.dot(t3[...], mixed[...], preferred_element_type=jnp.float32).astype(back.dtype)

    exchange(3, "lat", lat, lat_count, lambda p: back.at[aligned(p, 32)], rows.at[lat])
    build(3, t4)
    arrived(3, rows)

    exchange(4, "lon", lon, lon_count, lambda p: rows.at[:, aligned(p, 2)], waves.at[lon])
    arrived(4, waves)
    filtered = jnp.dot(
        t4[...], waves.reshape(t4.shape[1], 128)[...], preferred_element_type=jnp.float32
    )
    field[...] = (filtered * (2.0 * norm)).astype(field.dtype)

    exchange(5, "lon", lon, lon_count, lambda p: field.at[aligned(p, cells)], out_ref.at[lon])
    arrived(5, out_ref)

    for stage, (buffer, count) in enumerate(
        ((line, lon_count), (line, lon_count), (line, lat_count), (line, lat_count), (line, lon_count), (line, lon_count))
    ):
        sent = line.shape[0] // count * (count - 1)
        left = line.at[pl.ds(0, sent)]
        pltpu.make_async_copy(left, left, send_sem.at[stage]).wait()


def body(mesh, features, w_first, bias_first, w_second, bias_second):
    lat_rows, lon_cells, channels = features.shape
    lat_count, lon_count = mesh.shape["lat"], mesh.shape["lon"]
    total_lat, total_lon = lat_rows * lat_count, lon_cells * lon_count
    bases = jnp.asarray(table_bases(total_lat, total_lon))
    any_space = pl.BlockSpec(memory_space=pl.ANY)
    half = jnp.bfloat16
    waves_own = total_lon // 2 // lon_count
    flat = pltpu.VMEM((total_lon, channels), half)
    filtered = pl.pallas_call(
        functools.partial(mixer_kernel, lat_count, lon_count),
        out_shape=jax.ShapeDtypeStruct((lat_rows, lon_cells, channels), half),
        in_specs=[any_space] * 6,
        out_specs=any_space,
        scratch_shapes=[
            pltpu.VMEM(a.shape, a.dtype)
            for a in (bases, w_first, bias_first, w_second, bias_second)
        ]
        + [
            pltpu.VMEM((total_lon, total_lon), half),
            pltpu.VMEM((2 * total_lat, 2 * total_lat), half),
            pltpu.VMEM((2 * total_lat, 2 * total_lat), half),
            pltpu.VMEM((total_lon, total_lon), half),
            flat,
            flat,
            pltpu.VMEM((lon_count, 2 * waves_own, channels), half),
            pltpu.VMEM((lat_count, lat_rows, 2, channels), half),
            pltpu.VMEM((2 * total_lat, channels), half),
            pltpu.VMEM((2 * total_lat, channels), half),
            pltpu.VMEM((lat_count, 2 * lat_rows, channels), half),
            pltpu.VMEM((lon_count, waves_own, 2, channels), half),
            flat,
            pltpu.SemaphoreType.DMA((6,)),
            pltpu.SemaphoreType.DMA((6,)),
            pltpu.SemaphoreType.DMA((8,)),
        ],
        compiler_params=pltpu.CompilerParams(
            collective_id=0, has_side_effects=True, vmem_limit_bytes=60 * 2**20
        ),
    )(features, bases, w_first, bias_first, w_second, bias_second)
    return (features.astype(jnp.float32) + filtered.astype(jnp.float32)).astype(features.dtype)


def solution(mesh):
    in_specs = (P("lat", "lon", None), P(), P(), P(), P())
    out_specs = P("lat", "lon", None)
    return jax.shard_map(
        functools.partial(body, mesh),
        mesh=mesh,
        in_specs=in_specs,
        out_specs=out_specs,
        check_vma=False,
    )
```

```python
import functools
import math

import jax
import jax.numpy as jnp
import numpy as np
from jax import lax
from jax.experimental import pallas as pl
from jax.experimental.pallas import tpu as pltpu
from jax.sharding import PartitionSpec as P

shrink_level = 0.01
MESH = pl.DeviceIdType.MESH


def wave(turn, length):
    angle = (turn % length) * (2.0 * math.pi / length)
    return np.cos(angle), np.sin(angle)


def table_bases(total_lat, total_lon):
    waves = np.arange(total_lon // 2)
    cells = np.arange(total_lon)
    lats = np.arange(total_lat)
    group = np.arange(32)
    fine = np.arange(16)
    out = []
    c, s = wave(16 * np.outer(group, cells), total_lon)
    pc, ps = wave(np.outer(fine, cells), total_lon)
    p = np.stack([pc, -ps], axis=1).reshape(32, -1)
    q = np.stack([-ps, -pc], axis=1).reshape(32, -1)
    out.append((c, s, p, q))
    c, s = wave(16 * np.outer(group, np.repeat(lats, 2)), total_lat)
    pc, ps = wave(np.outer(fine, lats), total_lat)
    p = np.stack([np.stack([pc, ps], 2), np.stack([-ps, pc], 2)]).reshape(32, -1)
    q = np.stack([np.stack([-ps, pc], 2), np.stack([-pc, -ps], 2)]).reshape(32, -1)
    out.append((c, s, p, q))
    c, s = wave(16 * np.outer(group, np.tile(lats, 2)), total_lat)
    pc, ps = wave(np.outer(fine, lats), total_lat)
    p = np.stack([np.stack([pc, -ps], 1), np.stack([ps, pc], 1)], 1).reshape(32, -1)
    q = np.stack([np.stack([-ps, -pc], 1), np.stack([pc, -ps], 1)], 1).reshape(32, -1)
    out.append((c, s, p, q))
    c, s = wave(32 * np.outer(group, np.repeat(waves, 2)), total_lon)
    pc, ps = wave(np.outer(group, waves), total_lon)
    p = np.stack([pc, -ps], axis=2).reshape(32, -1)
    q = np.stack([-ps, -pc], axis=2).reshape(32, -1)
    out.append((c, s, p, q))
    return np.stack([np.stack(kind) for kind in out]).astype(np.float32)


def aligned(index, size):
    return pl.ds(pl.multiple_of(index * size, size), size)


def far_first(step):
    half = (step + 1) // 2
    return lax.rem(4 + half - 2 * half * lax.rem(step, 2) + 8, 8)


def mixer_kernel(
    x_ref,
    bases_hbm,
    w1_hbm,
    b1_hbm,
    w2_hbm,
    b2_hbm,
    landed,
    bases,
    w1_ref,
    b1_ref,
    w2_ref,
    b2_ref,
    t1,
    t2,
    t3,
    t4,
    swap,
    line,
    spec,
    part,
    by_wave,
    column,
    mixed,
    back,
    rows,
    by_row,
    waves,
    field,
    send_sem,
    recv_sem,
    table_sem,
):
    lat = lax.axis_index("lat")
    lon = lax.axis_index("lon")
    x_hi, y, core = lat // 16, lax.rem(lat // 2, 8), lax.rem(lat, 2)
    z, x_lo = lon // 2, lax.rem(lon, 2)
    z_hi = lon // 8
    norm = 1.0 / math.sqrt(t2.shape[0] // 2 * t1.shape[1])

    fetches = [
        pltpu.make_async_copy(bases_hbm.at[n], bases.at[n], table_sem.at[n]) for n in range(4)
    ] + [
        pltpu.make_async_copy(hbm, vmem, table_sem.at[4 + n])
        for n, (hbm, vmem) in enumerate(
            ((w1_hbm, w1_ref), (b1_hbm, b1_ref), (w2_hbm, w2_ref), (b2_hbm, b2_ref))
        )
    ]
    for copy in fetches:
        copy.start()

    def build(n, table):
        fetches[n].wait()
        first = (1 - x_hi) if n == 0 else (1 - z_hi)

        def group(g, _):
            c = bases[n, 0, pl.ds(g, 1), :]
            s = bases[n, 1, pl.ds(g, 1), :]
            if n in (1, 2):
                for half in range(2):
                    near = pl.ds(16 * half, 16)
                    block = c * bases[n, 2, near, :] + s * bases[n, 3, near, :]
                    turn = half if n == 1 else lax.rem(half + first, 2)
                    start = pl.multiple_of(512 * turn + 16 * g, 16)
                    table[pl.ds(start, 16), :] = block.astype(table.dtype)
            else:
                block = c * bases[n, 2] + s * bases[n, 3]
                start = 32 * g if n == 3 else 512 * lax.rem(g + first, 2) + 32 * (g // 2)
                table[pl.ds(pl.multiple_of(start, 32), 32), :] = block.astype(table.dtype)
            return 0

        lax.fori_loop(0, 32, group, 0)

    barrier = pltpu.get_barrier_semaphore()

    def greet_lon(step, _):
        peer = lax.rem(lon + step, 16)
        pl.semaphore_signal(barrier, inc=1, device_id={"lon": peer}, device_id_type=MESH)
        return 0

    def greet_lat(step, _):
        peer = lax.rem(lat + step, 32)
        pl.semaphore_signal(barrier, inc=1, device_id={"lat": peer}, device_id_type=MESH)
        return 0

    lax.fori_loop(1, 16, greet_lon, 0)
    lax.fori_loop(1, 32, greet_lat, 0)
    pl.semaphore_wait(barrier, 46)

    def lon_peer(step):
        return lax.rem(z + far_first(step // 2), 8) * 2 + lax.rem(x_lo + 1 + step, 2)

    def lat_peer(other, step):
        place = lax.rem(y + far_first(step // 2), 8) * 2 + lax.rem(core + 1 + step, 2)
        return lax.rem(x_hi + other, 2) * 16 + place

    def push(slot, axis, steps, peer_of, source, target):
        def send(step, _):
            peer = peer_of(step)
            pltpu.make_async_remote_copy(
                src_ref=source(peer),
                dst_ref=target,
                send_sem=send_sem.at[slot],
                recv_sem=recv_sem.at[slot],
                device_id={axis: peer},
                device_id_type=MESH,
            ).start()
            return 0

        lax.fori_loop(steps[0], steps[1], send, 0)

    def keep(slot, source, target):
        pltpu.make_async_copy(source, target, recv_sem.at[slot]).start()

    def arrived(slot, landing):
        pltpu.make_async_copy(landing, landing, recv_sem.at[slot]).wait()

    def regroup(block):
        flat = block.reshape(256, block.shape[-1])
        return jnp.dot(swap[...], flat, preferred_element_type=jnp.float32).astype(flat.dtype)

    keep(0, x_ref.at[lon], line.at[aligned(lon, 64)])
    push(0, "lon", (0, 15), lon_peer, lambda p: x_ref.at[p], line.at[aligned(lon, 64)])
    build(0, t1)
    row = lax.broadcasted_iota(jnp.int32, swap.shape, 0)
    col = lax.broadcasted_iota(jnp.int32, swap.shape, 1)
    source = (row % 32) // 2 * 16 + row // 32 * 2 + row % 2
    swap[...] = jnp.where(col == source, 1.0, 0.0).astype(swap.dtype)
    arrived(0, line)

    for turn in range(2):
        height = pl.ds(512 * turn, 512)
        spec[height, :] = jnp.dot(
            t1[height, :], line[...], preferred_element_type=jnp.float32
        ).astype(spec.dtype)
        keep(1 + turn, spec.at[pl.ds(pl.multiple_of(512 * turn + 32 * lon, 32), 32)], part.at[turn, lon])
        push(
            1 + turn,
            "lon",
            (0, 15),
            lon_peer,
            lambda p, turn=turn: spec.at[pl.ds(pl.multiple_of(512 * turn + 32 * p, 32), 32)],
            part.at[turn, lon],
        )
    build(1, t2)

    for turn in range(2):
        arrived(1 + turn, part.at[turn])
        for eight in range(2):
            block = regroup(part[turn, :, 16 * eight : 16 * eight + 16, :])
            by_wave[turn, 8 * eight : 8 * eight + 8] = block.reshape(8, 32, block.shape[-1])
        if turn == 1:
            keep(3, by_wave.at[turn, lax.rem(lat, 16)], column.at[aligned(lat, 32)])
        push(
            3,
            "lat",
            (0, 16 - turn),
            functools.partial(lat_peer, 1 - turn),
            lambda p, turn=turn: by_wave.at[turn, lax.rem(p, 16)],
            column.at[aligned(lat, 32)],
        )
    build(2, t3)
    for copy in fetches[4:]:
        copy.wait()
    arrived(3, column)
    spectrum = jnp.dot(t2[...], column[...], preferred_element_type=jnp.float32)
    spectrum = (spectrum * norm).astype(jnp.bfloat16)

    def product(left_re, left_im, w_ref):
        w_re, w_im = w_ref[0, 0], w_ref[1, 0]
        re = jnp.dot(left_re, w_re, preferred_element_type=jnp.float32) - jnp.dot(
            left_im, w_im, preferred_element_type=jnp.float32
        )
        im = jnp.dot(left_im, w_re, preferred_element_type=jnp.float32) + jnp.dot(
            left_re, w_im, preferred_element_type=jnp.float32
        )
        return re, im

    def shrink(v):
        return jnp.maximum(v - shrink_level, 0.0) + jnp.minimum(v + shrink_level, 0.0)

    hid_re, hid_im = product(spectrum[:512], spectrum[512:], w1_ref)
    act_re = jnp.maximum(hid_re + b1_ref[0], 0.0).astype(jnp.bfloat16)
    act_im = jnp.maximum(hid_im + b1_ref[1], 0.0).astype(jnp.bfloat16)
    out_re, out_im = product(act_re, act_im, w2_ref)
    weight = jnp.where(lat + lon == 0, 0.5, 1.0)
    mixed[:512] = (shrink(out_re + b2_ref[0]) * weight).astype(jnp.bfloat16)
    mixed[512:] = (shrink(out_im + b2_ref[1]) * weight).astype(jnp.bfloat16)

    for turn in range(2):
        height = pl.ds(512 * turn, 512)
        back[height, :] = jnp.dot(
            t3[height, :], mixed[...], preferred_element_type=jnp.float32
        ).astype(back.dtype)
        keep(4 + turn, back.at[pl.ds(pl.multiple_of(512 * turn + 16 * lat, 16), 16)], rows.at[turn, lat])
        for near in range(2):
            push(
                4 + turn,
                "lat",
                (0, 16 - near),
                functools.partial(lat_peer, 1 - near),
                lambda p, turn=turn: back.at[pl.ds(pl.multiple_of(512 * turn + 16 * p, 16), 16)],
                rows.at[turn, lat],
            )
    build(3, t4)

    for turn in range(2):
        arrived(4 + turn, rows.at[turn])
        for half in range(2):
            block = regroup(rows[turn, 16 * half : 16 * half + 16])
            by_row[turn, :, 32 * half : 32 * half + 32, :] = block.reshape(8, 32, block.shape[-1])
        if turn == 1:
            keep(6, by_row.at[turn, lax.rem(lon, 8)], waves.at[aligned(lon, 64)])
        push(
            6,
            "lon",
            (turn, 8),
            lambda step, turn=turn: lax.rem(z_hi + 1 - turn, 2) * 8 + lax.rem(lon + step, 8),
            lambda p, turn=turn: by_row.at[turn, lax.rem(p, 8)],
            waves.at[aligned(lon, 64)],
        )
    arrived(6, waves)
    filtered = jnp.dot(t4[...], waves[...], preferred_element_type=jnp.float32)
    field[...] = (filtered * (2.0 * norm)).astype(field.dtype)

    keep(7, field.at[aligned(lon, 64)], landed.at[lon])
    push(7, "lon", (0, 15), lon_peer, lambda p: field.at[aligned(p, 64)], landed.at[lon])
    arrived(7, landed)

    for slot, sent in enumerate((960, 480, 480, 992, 496, 496, 960, 960)):
        left = line.at[pl.ds(0, sent)]
        pltpu.make_async_copy(left, left, send_sem.at[slot]).wait()


def body(features, w_first, bias_first, w_second, bias_second):
    lat_rows, lon_cells, channels = features.shape
    lat_count, lon_count = lax.axis_size("lat"), lax.axis_size("lon")
    total_lat, total_lon = lat_rows * lat_count, lon_cells * lon_count
    bases = jnp.asarray(table_bases(total_lat, total_lon))
    hbm = pl.BlockSpec(memory_space=pltpu.HBM)
    half = jnp.bfloat16
    flat = pltpu.VMEM((1024, channels), half)
    table = pltpu.VMEM((1024, 1024), half)
    filtered = pl.pallas_call(
        mixer_kernel,
        out_shape=jax.ShapeDtypeStruct((lat_rows, lon_cells, channels), half),
        in_specs=[hbm] * 6,
        out_specs=pl.BlockSpec(memory_space=pltpu.VMEM),
        scratch_shapes=[
            pltpu.VMEM(a.shape, a.dtype)
            for a in (bases, w_first, bias_first, w_second, bias_second)
        ]
        + [table] * 4
        + [
            pltpu.VMEM((256, 256), half),
            flat,
            flat,
            pltpu.VMEM((2, 16, 32, channels), half),
            pltpu.VMEM((2, 16, 32, channels), half),
            flat,
            flat,
            flat,
            pltpu.VMEM((2, 32, 16, channels), half),
            pltpu.VMEM((2, 8, 64, channels), half),
            flat,
            flat,
            pltpu.SemaphoreType.DMA((8,)),
            pltpu.SemaphoreType.DMA((8,)),
            pltpu.SemaphoreType.DMA((8,)),
        ],
        compiler_params=pltpu.CompilerParams(
            collective_id=0, has_side_effects=True, vmem_limit_bytes=40 * 2**20
        ),
    )(
        *(
            pltpu.with_memory_space_constraint(a, pltpu.HBM)
            for a in (features, bases, w_first, bias_first, w_second, bias_second)
        )
    )
    return (features.astype(jnp.float32) + filtered.astype(jnp.float32)).astype(features.dtype)


def solution(mesh):
    in_specs = (P("lat", "lon", None), P(), P(), P(), P())
    out_specs = P("lat", "lon", None)
    return jax.shard_map(
        body, mesh=mesh, in_specs=in_specs, out_specs=out_specs, check_vma=False
    )
```

```python
import functools
import math

import jax
import jax.numpy as jnp
import numpy as np
from jax import lax
from jax.experimental import pallas as pl
from jax.experimental.pallas import tpu as pltpu
from jax.sharding import PartitionSpec as P

shrink_level = 0.01
MESH = pl.DeviceIdType.MESH


def wave(turn, length):
    angle = (turn % length) * (2.0 * math.pi / length)
    return np.cos(angle), np.sin(angle)


def table_bases(total_lat, total_lon):
    waves = np.arange(total_lon // 2)
    cells = np.arange(total_lon)
    lats = np.arange(total_lat)
    group = np.arange(32)
    fine = np.arange(16)
    place, core = lats // 2, lats % 2
    row_y, row_z, row_hi, row_lo = place // 32, place // 4 % 8, place // 2 % 2, place % 2
    row = 16 * ((row_hi * 8 + row_y) * 2 + core) + 2 * row_z + row_lo
    out = []
    c, s = wave(16 * np.outer(group, cells), total_lon)
    pc, ps = wave(np.outer(fine, cells), total_lon)
    p = np.stack([pc, -ps], axis=1).reshape(32, -1)
    q = np.stack([-ps, -pc], axis=1).reshape(32, -1)
    out.append((c, s, p, q))
    c, s = wave(16 * np.outer(group, np.repeat(row, 2)), total_lat)
    pc, ps = wave(np.outer(fine, row), total_lat)
    p = np.stack([np.stack([pc, ps], 2), np.stack([-ps, pc], 2)]).reshape(32, -1)
    q = np.stack([np.stack([-ps, pc], 2), np.stack([-pc, -ps], 2)]).reshape(32, -1)
    out.append((c, s, p, q))
    c, s = wave(np.outer(row[::16], np.tile(lats, 2)), total_lat)
    pc, ps = wave(np.outer(row[:16], lats), total_lat)
    p = np.stack([np.stack([pc, -ps], 1), np.stack([ps, pc], 1)], 1).reshape(32, -1)
    q = np.stack([np.stack([-ps, -pc], 1), np.stack([pc, -ps], 1)], 1).reshape(32, -1)
    out.append((c, s, p, q))
    c, s = wave(32 * np.outer(group, np.repeat(waves, 2)), total_lon)
    pc, ps = wave(np.outer(group, waves), total_lon)
    p = np.stack([pc, -ps], axis=2).reshape(32, -1)
    q = np.stack([-ps, -pc], axis=2).reshape(32, -1)
    out.append((c, s, p, q))
    return np.stack([np.stack(kind) for kind in out]).astype(np.float32)


def wide_order():
    def hops(o):
        return min(o[0], 8 - o[0]) + min(o[1], 8 - o[1]) + 2 * o[2] + o[3]

    offsets = [(y, z, h, l) for y in range(8) for z in range(8) for h in range(2) for l in range(2)]
    return sorted(offsets[1:], key=lambda o: -hops(o))


def aligned(index, size):
    return pl.ds(pl.multiple_of(index * size, size), size)


def far_first(step):
    half = (step + 1) // 2
    return lax.rem(4 + half - 2 * half * lax.rem(step, 2) + 8, 8)


def mixer_kernel(
    x_ref,
    bases_hbm,
    w1_hbm,
    b1_hbm,
    w2_hbm,
    b2_hbm,
    landed,
    bases,
    w1_ref,
    b1_ref,
    w2_ref,
    b2_ref,
    t1,
    t2,
    t3,
    t4,
    swap,
    swap_back,
    line,
    spec,
    pair,
    by_place,
    column,
    mixed,
    back,
    wide,
    pair_back,
    waves,
    field,
    send_sem,
    recv_sem,
    table_sem,
):
    lat = lax.axis_index("lat")
    lon = lax.axis_index("lon")
    x_hi, y, core = lat // 16, lax.rem(lat // 2, 8), lax.rem(lat, 2)
    z, x_lo = lon // 2, lax.rem(lon, 2)
    z_hi = lon // 8
    norm = 1.0 / math.sqrt(t2.shape[0] // 2 * t1.shape[1])

    fetches = [
        pltpu.make_async_copy(bases_hbm.at[n], bases.at[n], table_sem.at[n]) for n in range(4)
    ] + [
        pltpu.make_async_copy(hbm, vmem, table_sem.at[4 + n])
        for n, (hbm, vmem) in enumerate(
            ((w1_hbm, w1_ref), (b1_hbm, b1_ref), (w2_hbm, w2_ref), (b2_hbm, b2_ref))
        )
    ]
    for copy in fetches:
        copy.start()

    def build(n, table):
        fetches[n].wait()

        def group(g, _):
            c = bases[n, 0, pl.ds(g, 1), :]
            s = bases[n, 1, pl.ds(g, 1), :]
            if n == 1:
                for part in range(2):
                    near = pl.ds(16 * part, 16)
                    block = c * bases[n, 2, near, :] + s * bases[n, 3, near, :]
                    start = pl.multiple_of(512 * part + 16 * g, 16)
                    table[pl.ds(start, 16), :] = block.astype(table.dtype)
            else:
                table[aligned(g, 32), :] = (c * bases[n, 2] + s * bases[n, 3]).astype(table.dtype)
            return 0

        lax.fori_loop(0, 32, group, 0)

    barrier = pltpu.get_barrier_semaphore()

    def greet_lon(step, _):
        peer = lax.rem(lon + step, 16)
        pl.semaphore_signal(barrier, inc=1, device_id={"lon": peer}, device_id_type=MESH)
        return 0

    def greet_lat(step, _):
        peer = lax.rem(lat + 2 * step, 32)
        pl.semaphore_signal(barrier, inc=1, device_id={"lat": peer}, device_id_type=MESH)
        return 0

    sibling = lat + 1 - 2 * core
    lax.fori_loop(1, 16, greet_lon, 0)
    lax.fori_loop(1, 16, greet_lat, 0)
    pl.semaphore_signal(barrier, inc=1, device_id={"lat": sibling}, device_id_type=MESH)
    pl.semaphore_wait(barrier, 31)

    def lon_peer(step):
        return lax.rem(z + far_first(step // 2), 8) * 2 + lax.rem(x_lo + 1 + step, 2)

    def push(slot, axis, steps, peer_of, source, target):
        def send(step, _):
            peer = peer_of(step)
            pltpu.make_async_remote_copy(
                src_ref=source(peer),
                dst_ref=target,
                send_sem=send_sem.at[slot],
                recv_sem=recv_sem.at[slot],
                device_id={axis: peer},
                device_id_type=MESH,
            ).start()
            return 0

        lax.fori_loop(steps[0], steps[1], send, 0)

    def keep(slot, source, target):
        pltpu.make_async_copy(source, target, recv_sem.at[slot]).start()

    def arrived(slot, landing):
        pltpu.make_async_copy(landing, landing, recv_sem.at[slot]).wait()

    def to_sibling(slot, source, target):
        pltpu.make_async_remote_copy(
            src_ref=source,
            dst_ref=target,
            send_sem=send_sem.at[slot],
            recv_sem=recv_sem.at[slot],
            device_id={"lat": sibling},
            device_id_type=MESH,
        ).start()

    ys = [lax.rem(y + step, 8) for step in range(8)]
    zs = [lax.rem(z + step, 8) for step in range(8)]
    his = [x_hi, 1 - x_hi]
    los = [x_lo, 1 - x_lo]
    place = ((y * 8 + z) * 2 + x_hi) * 2 + x_lo

    def to_chips(slot, source, landing):
        keep(slot, source.at[aligned(place, 4)], landing.at[aligned(place, 4)])
        for dy, dz, dh, dl in wide_order():
            other = ((ys[dy] * 8 + zs[dz]) * 2 + his[dh]) * 2 + los[dl]
            pltpu.make_async_remote_copy(
                src_ref=source.at[aligned(other, 4)],
                dst_ref=landing.at[aligned(place, 4)],
                send_sem=send_sem.at[slot],
                recv_sem=recv_sem.at[slot],
                device_id={
                    "lat": (his[dh] * 8 + ys[dy]) * 2 + core,
                    "lon": zs[dz] * 2 + los[dl],
                },
                device_id_type=MESH,
            ).start()

    keep(0, x_ref.at[lon], line.at[aligned(lon, 64)])
    push(0, "lon", (0, 15), lon_peer, lambda p: x_ref.at[p], line.at[aligned(lon, 64)])
    build(0, t1)
    row = lax.broadcasted_iota(jnp.int32, swap.shape, 0)
    col = lax.broadcasted_iota(jnp.int32, swap.shape, 1)
    source = row // 2 % 2 * 128 + row // 4 * 2 + row % 2
    swap[...] = jnp.where(col == source, 1.0, 0.0).astype(swap.dtype)
    source = col // 2 % 2 * 128 + col // 4 * 2 + col % 2
    swap_back[...] = jnp.where(row == source, 1.0, 0.0).astype(swap.dtype)
    arrived(0, line)

    def half_of(which):
        rows = pl.ds(pl.multiple_of(512 * which, 512), 512)
        return jnp.dot(t1[rows, :], line[...], preferred_element_type=jnp.float32).astype(spec.dtype)

    spec[...] = half_of(1 - core)
    to_sibling(1, spec, pair.at[core])
    pair[core] = half_of(core)
    arrived(1, spec)

    for block in range(4):
        both = pair[:, 128 * block : 128 * block + 128, :].reshape(256, -1)
        both = jnp.dot(swap[...], both, preferred_element_type=jnp.float32)
        by_place[256 * block : 256 * block + 256, :] = both.astype(by_place.dtype)
    to_chips(2, by_place, column)
    build(1, t2)
    build(2, t3)
    for copy in fetches[4:]:
        copy.wait()
    arrived(2, column)
    spectrum = jnp.dot(t2[...], column[...], preferred_element_type=jnp.float32)
    spectrum = (spectrum * norm).astype(jnp.bfloat16)

    def product(left_re, left_im, w_ref):
        w_re, w_im = w_ref[0, 0], w_ref[1, 0]
        re = jnp.dot(left_re, w_re, preferred_element_type=jnp.float32) - jnp.dot(
            left_im, w_im, preferred_element_type=jnp.float32
        )
        im = jnp.dot(left_im, w_re, preferred_element_type=jnp.float32) + jnp.dot(
            left_re, w_im, preferred_element_type=jnp.float32
        )
        return re, im

    def shrink(v):
        return jnp.maximum(v - shrink_level, 0.0) + jnp.minimum(v + shrink_level, 0.0)

    hid_re, hid_im = product(spectrum[:512], spectrum[512:], w1_ref)
    act_re = jnp.maximum(hid_re + b1_ref[0], 0.0).astype(jnp.bfloat16)
    act_im = jnp.maximum(hid_im + b1_ref[1], 0.0).astype(jnp.bfloat16)
    out_re, out_im = product(act_re, act_im, w2_ref)
    weight = jnp.where(lat + lon == 0, 0.5, 1.0)
    mixed[:512] = (shrink(out_re + b2_ref[0]) * weight).astype(jnp.bfloat16)
    mixed[512:] = (shrink(out_im + b2_ref[1]) * weight).astype(jnp.bfloat16)

    back[...] = jnp.dot(t3[...], mixed[...], preferred_element_type=jnp.float32).astype(back.dtype)
    to_chips(3, back, wide)
    build(3, t4)
    arrived(3, wide)

    for block in range(4):
        both = wide[256 * block : 256 * block + 256, :]
        both = jnp.dot(swap_back[...], both, preferred_element_type=jnp.float32)
        both = both.astype(wide.dtype).reshape(2, 128, -1)
        pair_back[:, 128 * block : 128 * block + 128, :] = both
    to_sibling(4, pair_back.at[1 - core], waves)

    def part_of(half, which, operand):
        rows = pl.ds(pl.multiple_of(512 * half, 512), 512)
        columns = pl.ds(pl.multiple_of(512 * which, 512), 512)
        return jnp.dot(t4[rows, columns], operand, preferred_element_type=jnp.float32)

    far = 1 - z_hi
    held = [part_of(half, core, pair_back[core]) for half in (far, z_hi)]
    arrived(4, waves)
    for turn, half in enumerate((far, z_hi)):
        filtered = held[turn] + part_of(half, 1 - core, waves[...])
        field[512 * turn : 512 * turn + 512, :] = (filtered * (2.0 * norm)).astype(field.dtype)

        def block_of(peer, turn=turn):
            return field.at[pl.ds(pl.multiple_of(512 * turn + 64 * lax.rem(peer, 8), 64), 64)]

        if turn == 1:
            keep(5, block_of(lon), landed.at[lon])
        push(
            5,
            "lon",
            (turn, 8),
            lambda step, half=half: half * 8 + lax.rem(lon + step, 8),
            block_of,
            landed.at[lon],
        )
    arrived(5, landed)

    for slot, sent in enumerate((960, 512, 1020, 1020, 512, 960)):
        left = line.at[pl.ds(0, sent)]
        pltpu.make_async_copy(left, left, send_sem.at[slot]).wait()


def body(features, w_first, bias_first, w_second, bias_second):
    lat_rows, lon_cells, channels = features.shape
    lat_count, lon_count = lax.axis_size("lat"), lax.axis_size("lon")
    total_lat, total_lon = lat_rows * lat_count, lon_cells * lon_count
    bases = jnp.asarray(table_bases(total_lat, total_lon))
    hbm = pl.BlockSpec(memory_space=pltpu.HBM)
    half = jnp.bfloat16
    flat = pltpu.VMEM((1024, channels), half)
    table = pltpu.VMEM((1024, 1024), half)
    filtered = pl.pallas_call(
        mixer_kernel,
        out_shape=jax.ShapeDtypeStruct((lat_rows, lon_cells, channels), half),
        in_specs=[hbm] * 6,
        out_specs=pl.BlockSpec(memory_space=pltpu.VMEM),
        scratch_shapes=[
            pltpu.VMEM(a.shape, a.dtype)
            for a in (bases, w_first, bias_first, w_second, bias_second)
        ]
        + [table] * 4
        + [
            pltpu.VMEM((256, 256), half),
            pltpu.VMEM((256, 256), half),
            flat,
            pltpu.VMEM((512, channels), half),
            pltpu.VMEM((2, 512, channels), half),
            flat,
            flat,
            flat,
            flat,
            flat,
            pltpu.VMEM((2, 512, channels), half),
            pltpu.VMEM((512, channels), half),
            flat,
            pltpu.SemaphoreType.DMA((6,)),
            pltpu.SemaphoreType.DMA((6,)),
            pltpu.SemaphoreType.DMA((8,)),
        ],
        compiler_params=pltpu.CompilerParams(
            collective_id=0, has_side_effects=True, vmem_limit_bytes=40 * 2**20
        ),
    )(
        *(
            pltpu.with_memory_space_constraint(a, pltpu.HBM)
            for a in (features, bases, w_first, bias_first, w_second, bias_second)
        )
    )
    return (features.astype(jnp.float32) + filtered.astype(jnp.float32)).astype(features.dtype)


def solution(mesh):
    in_specs = (P("lat", "lon", None), P(), P(), P(), P())
    out_specs = P("lat", "lon", None)
    return jax.shard_map(
        body, mesh=mesh, in_specs=in_specs, out_specs=out_specs, check_vma=False
    )
```

```python
import functools
import math

import jax
import jax.numpy as jnp
import numpy as np
from jax import lax
from jax.experimental import pallas as pl
from jax.experimental.pallas import tpu as pltpu
from jax.sharding import PartitionSpec as P

shrink_level = 0.01
MESH = pl.DeviceIdType.MESH


def wave(turn, length):
    angle = (turn % length) * (2.0 * math.pi / length)
    return np.cos(angle), np.sin(angle)


def table_bases(total_lat, total_lon):
    cells = np.arange(total_lon // 2)
    fine = np.arange(16)
    place, core = np.arange(total_lat // 2) // 2, np.arange(total_lat // 2) % 2
    row = 16 * (place // 16 * 2 + core) + place % 16
    lon_waves = np.arange(total_lon // 2).reshape(-1, 2).T.reshape(-1)
    lat_waves = np.arange(total_lat).reshape(-1, 2).T.reshape(2, -1)
    c, s = wave(np.outer(lon_waves[::16], cells), total_lon)
    pc, ps = wave(2 * np.outer(fine, cells), total_lon)
    p = np.stack([pc, -ps], axis=1).reshape(32, -1)
    q = np.stack([-ps, -pc], axis=1).reshape(32, -1)
    narrow = [(c, s, p, q)]
    c, s = wave(np.outer(lat_waves.reshape(-1)[::16], np.repeat(row, 2)), total_lat)
    pc, ps = wave(2 * np.outer(fine, row), total_lat)
    p = np.stack([np.stack([pc, ps], 2), np.stack([-ps, pc], 2)]).reshape(32, -1)
    q = np.stack([np.stack([-ps, pc], 2), np.stack([-pc, -ps], 2)]).reshape(32, -1)
    narrow.append((c, s, p, q))
    columns = np.stack([lat_waves, lat_waves], axis=1).reshape(-1)
    c, s = wave(np.outer(np.tile(row[::16], 2), columns), total_lat)
    pc, ps = wave(np.outer(row[:16], lat_waves), total_lat)
    pc, ps = pc.reshape(16, 2, -1), ps.reshape(16, 2, -1)
    p = np.stack([np.stack([pc, -ps], 2), np.stack([ps, pc], 2)], 1).reshape(32, -1)
    q = np.stack([np.stack([-ps, -pc], 2), np.stack([pc, -ps], 2)], 1).reshape(32, -1)
    broad = [(c, s, p, q)]
    c, s = wave(np.outer(np.tile(cells[::32], 2), np.repeat(lon_waves, 2)), total_lon)
    pc, ps = wave(np.outer(np.arange(32), lon_waves), total_lon)
    p = np.stack([pc, -ps], axis=2).reshape(32, -1)
    q = np.stack([-ps, -pc], axis=2).reshape(32, -1)
    broad.append((c, s, p, q))
    return [np.array(t).astype(np.float32) for t in (narrow, broad)]


def wide_order():
    def hops(o):
        return min(o[0], 8 - o[0]) + min(o[1], 8 - o[1]) + 2 * o[2] + o[3]

    offsets = [(y, z, h, l) for y in range(8) for z in range(8) for h in range(2) for l in range(2)]
    return sorted(offsets[1:], key=lambda o: -hops(o))


def aligned(index, size):
    return pl.ds(pl.multiple_of(index * size, size), size)


def far_first(step):
    half = (step + 1) // 2
    return lax.rem(4 + half - 2 * half * lax.rem(step, 2) + 8, 8)


def mixer_kernel(
    x_ref,
    narrow_hbm,
    broad_hbm,
    w1_hbm,
    b1_hbm,
    w2_hbm,
    b2_hbm,
    landed,
    narrow,
    broad,
    w1_ref,
    b1_ref,
    w2_ref,
    b2_ref,
    t1,
    t2,
    t3,
    t4,
    swap,
    swap_back,
    mix1,
    mix2,
    line,
    spec,
    pair,
    by_place,
    column,
    mixed,
    back,
    wide,
    pair_back,
    waves,
    field,
    send_sem,
    recv_sem,
    table_sem,
):
    lat = lax.axis_index("lat")
    lon = lax.axis_index("lon")
    x_hi, y, core = lat // 16, lax.rem(lat // 2, 8), lax.rem(lat, 2)
    z, x_lo = lon // 2, lax.rem(lon, 2)
    z_hi = lon // 8
    norm = 1.0 / math.sqrt(t2.shape[0] // 2 * t4.shape[1])

    fetches = [
        pltpu.make_async_copy(hbm.at[n], vmem.at[n], table_sem.at[2 * m + n])
        for m, (hbm, vmem) in enumerate(((narrow_hbm, narrow), (broad_hbm, broad)))
        for n in range(2)
    ] + [
        pltpu.make_async_copy(hbm, vmem, table_sem.at[4 + n])
        for n, (hbm, vmem) in enumerate(
            ((w1_hbm, w1_ref), (b1_hbm, b1_ref), (w2_hbm, w2_ref), (b2_hbm, b2_ref))
        )
    ]
    for copy in fetches:
        copy.start()

    def build(n, table):
        fetches[n].wait()
        bases = (narrow if n < 2 else broad).at[n % 2]

        def group(g, _):
            c = bases[0, pl.ds(g, 1), :]
            s = bases[1, pl.ds(g, 1), :]
            if n == 1:
                for part in range(2):
                    near = pl.ds(16 * part, 16)
                    block = c * bases[2, near, :] + s * bases[3, near, :]
                    start = 512 * (g // 16) + 256 * part + 16 * lax.rem(g, 16)
                    table[pl.ds(pl.multiple_of(start, 16), 16), :] = block.astype(table.dtype)
            else:
                table[aligned(g, 32), :] = (c * bases[2] + s * bases[3]).astype(table.dtype)
            return 0

        lax.fori_loop(0, 32 if n < 2 else 16, group, 0)

    def join(w_ref, mix):
        mix[:128, :128] = w_ref[0, 0]
        mix[:128, 128:] = w_ref[1, 0]
        mix[128:, :128] = -w_ref[1, 0]
        mix[128:, 128:] = w_ref[0, 0]

    barrier = pltpu.get_barrier_semaphore()

    def greet_lon(step, _):
        peer = lax.rem(lon + step, 16)
        pl.semaphore_signal(barrier, inc=1, device_id={"lon": peer}, device_id_type=MESH)
        return 0

    def greet_lat(step, _):
        peer = lax.rem(lat + 2 * step, 32)
        pl.semaphore_signal(barrier, inc=1, device_id={"lat": peer}, device_id_type=MESH)
        return 0

    sibling = lat + 1 - 2 * core
    lax.fori_loop(1, 16, greet_lon, 0)
    lax.fori_loop(1, 16, greet_lat, 0)
    pl.semaphore_signal(barrier, inc=1, device_id={"lat": sibling}, device_id_type=MESH)
    pl.semaphore_wait(barrier, 31)

    def lon_peer(step):
        return lax.rem(z + far_first(step // 2), 8) * 2 + lax.rem(x_lo + 1 + step, 2)

    def push(slot, axis, steps, peer_of, source, target):
        def send(step, _):
            peer = peer_of(step)
            pltpu.make_async_remote_copy(
                src_ref=source(peer),
                dst_ref=target,
                send_sem=send_sem.at[slot],
                recv_sem=recv_sem.at[slot],
                device_id={axis: peer},
                device_id_type=MESH,
            ).start()
            return 0

        lax.fori_loop(steps[0], steps[1], send, 0)

    def keep(slot, source, target):
        pltpu.make_async_copy(source, target, recv_sem.at[slot]).start()

    def arrived(slot, landing):
        pltpu.make_async_copy(landing, landing, recv_sem.at[slot]).wait()

    def to_sibling(slot, source, target):
        pltpu.make_async_remote_copy(
            src_ref=source,
            dst_ref=target,
            send_sem=send_sem.at[slot],
            recv_sem=recv_sem.at[slot],
            device_id={"lat": sibling},
            device_id_type=MESH,
        ).start()

    ys = [lax.rem(y + step, 8) for step in range(8)]
    zs = [lax.rem(z + step, 8) for step in range(8)]
    his = [x_hi, 1 - x_hi]
    los = [x_lo, 1 - x_lo]
    place = ((x_hi * 8 + y) * 8 + z) * 2 + x_lo

    def to_chips(slot, source, landing):
        keep(slot, source.at[aligned(place, 4)], landing.at[aligned(place, 4)])
        for dy, dz, dh, dl in wide_order():
            other = ((his[dh] * 8 + ys[dy]) * 8 + zs[dz]) * 2 + los[dl]
            pltpu.make_async_remote_copy(
                src_ref=source.at[aligned(other, 4)],
                dst_ref=landing.at[aligned(place, 4)],
                send_sem=send_sem.at[slot],
                recv_sem=recv_sem.at[slot],
                device_id={
                    "lat": (his[dh] * 8 + ys[dy]) * 2 + core,
                    "lon": zs[dz] * 2 + los[dl],
                },
                device_id_type=MESH,
            ).start()

    keep(0, x_ref.at[lon], line.at[aligned(lon, 64)])
    push(0, "lon", (0, 15), lon_peer, lambda p: x_ref.at[p], line.at[aligned(lon, 64)])
    build(0, t1)
    row = lax.broadcasted_iota(jnp.int32, swap.shape, 0)
    col = lax.broadcasted_iota(jnp.int32, swap.shape, 1)
    source = row // 2 % 2 * 128 + row // 4 * 2 + row % 2
    swap[...] = jnp.where(col == source, 1.0, 0.0).astype(swap.dtype)
    source = col // 2 % 2 * 128 + col // 4 * 2 + col % 2
    swap_back[...] = jnp.where(row == source, 1.0, 0.0).astype(swap.dtype)
    arrived(0, line)

    def fold(block, sign):
        return (block[:512].astype(jnp.float32) + sign * block[512:].astype(jnp.float32)).astype(
            block.dtype
        )

    def half_of(parity):
        rows = pl.ds(pl.multiple_of(512 * parity, 512), 512)
        operand = fold(line[...], (1 - 2 * parity).astype(jnp.float32))
        return jnp.dot(t1[rows, :], operand, preferred_element_type=jnp.float32).astype(spec.dtype)

    spec[...] = half_of(1 - core)
    to_sibling(1, spec, pair.at[core])
    pair[core] = half_of(core)
    arrived(1, spec)

    for block in range(4):
        both = pair[:, 128 * block : 128 * block + 128, :].reshape(256, -1)
        both = jnp.dot(swap[...], both, preferred_element_type=jnp.float32)
        by_place[256 * block : 256 * block + 256, :] = both.astype(by_place.dtype)
    to_chips(2, by_place, column)
    build(1, t2)
    build(2, t3)
    for copy in fetches[4:]:
        copy.wait()
    join(w1_ref, mix1)
    join(w2_ref, mix2)
    bias1 = jnp.concatenate([b1_ref[0], b1_ref[1]], axis=1)
    bias2 = jnp.concatenate([b2_ref[0], b2_ref[1]], axis=1)
    weight = jnp.where(lat + lon == 0, 0.5, 1.0)
    arrived(2, column)

    def shrink(v):
        return jnp.maximum(v - shrink_level, 0.0) + jnp.minimum(v + shrink_level, 0.0)

    for parity in range(2):
        rows = pl.ds(512 * parity, 512)
        spectrum = jnp.dot(
            t2[rows, :], fold(column[...], 1.0 - 2.0 * parity), preferred_element_type=jnp.float32
        )
        spectrum = (spectrum * norm).astype(jnp.bfloat16)
        spectrum = jnp.concatenate([spectrum[:256], spectrum[256:]], axis=1)
        hidden = jnp.dot(spectrum, mix1[...], preferred_element_type=jnp.float32)
        hidden = jnp.maximum(hidden + bias1, 0.0).astype(jnp.bfloat16)
        result = jnp.dot(hidden, mix2[...], preferred_element_type=jnp.float32)
        result = (shrink(result + bias2) * weight).astype(jnp.bfloat16)
        mixed[512 * parity : 512 * parity + 256] = result[:, :128]
        mixed[512 * parity + 256 : 512 * parity + 512] = result[:, 128:]

    even = jnp.dot(t3[:, :512], mixed[:512], preferred_element_type=jnp.float32)
    odd = jnp.dot(t3[:, 512:], mixed[512:], preferred_element_type=jnp.float32)
    back[:512] = (even + odd).astype(back.dtype)
    back[512:] = (even - odd).astype(back.dtype)
    to_chips(3, back, wide)
    build(3, t4)
    arrived(3, wide)

    for block in range(4):
        both = wide[256 * block : 256 * block + 256, :]
        both = jnp.dot(swap_back[...], both, preferred_element_type=jnp.float32)
        both = both.astype(wide.dtype).reshape(2, 128, -1)
        pair_back[:, 128 * block : 128 * block + 128, :] = both
    to_sibling(4, pair_back.at[1 - core], waves)

    def part_of(parity, operand):
        columns = pl.ds(pl.multiple_of(512 * parity, 512), 512)
        return jnp.dot(t4[:, columns], operand, preferred_element_type=jnp.float32)

    held = part_of(core, pair_back[core])
    arrived(4, waves)
    fresh = part_of(1 - core, waves[...])
    for turn, half in enumerate((1 - z_hi, z_hi)):
        sign = (1 - 2 * half).astype(jnp.float32)
        scale = (1 - 2 * half * core).astype(jnp.float32) * (2.0 * norm)
        filtered = (held + sign * fresh) * scale
        field[512 * turn : 512 * turn + 512, :] = filtered.astype(field.dtype)

        def block_of(peer, turn=turn):
            return field.at[pl.ds(pl.multiple_of(512 * turn + 64 * lax.rem(peer, 8), 64), 64)]

        if turn == 1:
            keep(5, block_of(lon), landed.at[lon])
        push(
            5,
            "lon",
            (turn, 8),
            lambda step, half=half: half * 8 + lax.rem(lon + step, 8),
            block_of,
            landed.at[lon],
        )
    arrived(5, landed)

    for slot, sent in enumerate((960, 512, 1020, 1020, 512, 960)):
        left = line.at[pl.ds(0, sent)]
        pltpu.make_async_copy(left, left, send_sem.at[slot]).wait()


def body(features, w_first, bias_first, w_second, bias_second):
    lat_rows, lon_cells, channels = features.shape
    lat_count, lon_count = lax.axis_size("lat"), lax.axis_size("lon")
    total_lat, total_lon = lat_rows * lat_count, lon_cells * lon_count
    narrow, broad = (jnp.asarray(t) for t in table_bases(total_lat, total_lon))
    hbm = pl.BlockSpec(memory_space=pltpu.HBM)
    half = jnp.bfloat16
    flat = pltpu.VMEM((1024, channels), half)
    tables = [pltpu.VMEM(shape, half) for shape in [(1024, 512)] * 2 + [(512, 1024)] * 2]
    filtered = pl.pallas_call(
        mixer_kernel,
        out_shape=jax.ShapeDtypeStruct((lat_rows, lon_cells, channels), half),
        in_specs=[hbm] * 7,
        out_specs=pl.BlockSpec(memory_space=pltpu.VMEM),
        scratch_shapes=[
            pltpu.VMEM(a.shape, a.dtype)
            for a in (narrow, broad, w_first, bias_first, w_second, bias_second)
        ]
        + tables
        + [
            pltpu.VMEM((256, 256), half),
            pltpu.VMEM((256, 256), half),
            pltpu.VMEM((256, 256), half),
            pltpu.VMEM((256, 256), half),
            flat,
            pltpu.VMEM((512, channels), half),
            pltpu.VMEM((2, 512, channels), half),
            flat,
            flat,
            flat,
            flat,
            flat,
            pltpu.VMEM((2, 512, channels), half),
            pltpu.VMEM((512, channels), half),
            flat,
            pltpu.SemaphoreType.DMA((6,)),
            pltpu.SemaphoreType.DMA((6,)),
            pltpu.SemaphoreType.DMA((8,)),
        ],
        compiler_params=pltpu.CompilerParams(
            collective_id=0, has_side_effects=True, vmem_limit_bytes=40 * 2**20
        ),
    )(
        *(
            pltpu.with_memory_space_constraint(a, pltpu.HBM)
            for a in (features, narrow, broad, w_first, bias_first, w_second, bias_second)
        )
    )
    return (features.astype(jnp.float32) + filtered.astype(jnp.float32)).astype(features.dtype)


def solution(mesh):
    in_specs = (P("lat", "lon", None), P(), P(), P(), P())
    out_specs = P("lat", "lon", None)
    return jax.shard_map(
        body, mesh=mesh, in_specs=in_specs, out_specs=out_specs, check_vma=False
    )
```

```python
import functools
import math

import jax
import jax.numpy as jnp
import numpy as np
from jax import lax
from jax.experimental import pallas as pl
from jax.experimental.pallas import tpu as pltpu
from jax.sharding import PartitionSpec as P

shrink_level = 0.01
MESH = pl.DeviceIdType.MESH


def wave(turn, length):
    angle = (turn % length) * (2.0 * math.pi / length)
    return np.cos(angle), np.sin(angle)


def table_bases(total_lat, total_lon):
    cells = np.arange(total_lon // 2)
    fine = np.arange(16)
    place, core = np.arange(total_lat // 2) // 2, np.arange(total_lat // 2) % 2
    row = 16 * (place // 16 * 2 + core) + place % 16
    lon_waves = np.arange(total_lon // 2).reshape(-1, 2).T.reshape(-1)
    lat_waves = np.arange(total_lat).reshape(-1, 2).T.reshape(2, -1)
    c, s = wave(np.outer(lon_waves[::16], cells), total_lon)
    pc, ps = wave(2 * np.outer(fine, cells), total_lon)
    p = np.stack([pc, -ps], axis=1).reshape(32, -1)
    q = np.stack([-ps, -pc], axis=1).reshape(32, -1)
    narrow = [(c, s, p, q)]
    c, s = wave(np.outer(lat_waves.reshape(-1)[::16], np.repeat(row, 2)), total_lat)
    pc, ps = wave(2 * np.outer(fine, row), total_lat)
    p = np.stack([np.stack([pc, ps], 2), np.stack([-ps, pc], 2)]).reshape(32, -1)
    q = np.stack([np.stack([-ps, pc], 2), np.stack([-pc, -ps], 2)]).reshape(32, -1)
    narrow.append((c, s, p, q))
    columns = np.stack([lat_waves, lat_waves], axis=1).reshape(-1)
    c, s = wave(np.outer(np.tile(row[::16], 2), columns), total_lat)
    pc, ps = wave(np.outer(row[:16], lat_waves), total_lat)
    pc, ps = pc.reshape(16, 2, -1), ps.reshape(16, 2, -1)
    p = np.stack([np.stack([pc, -ps], 2), np.stack([ps, pc], 2)], 1).reshape(32, -1)
    q = np.stack([np.stack([-ps, -pc], 2), np.stack([pc, -ps], 2)], 1).reshape(32, -1)
    broad = [(c, s, p, q)]
    c, s = wave(np.outer(np.tile(cells[::32], 2), np.repeat(lon_waves, 2)), total_lon)
    pc, ps = wave(np.outer(np.arange(32), lon_waves), total_lon)
    p = np.stack([pc, -ps], axis=2).reshape(32, -1)
    q = np.stack([-ps, -pc], axis=2).reshape(32, -1)
    broad.append((c, s, p, q))
    return [np.array(t).astype(np.float32) for t in (narrow, broad)]


def wide_order():
    def hops(o):
        return min(o[0], 8 - o[0]) + min(o[1], 8 - o[1]) + 2 * o[2] + o[3]

    offsets = [(y, z, h, l) for y in range(8) for z in range(8) for h in range(2) for l in range(2)]
    return sorted(offsets[1:], key=lambda o: -hops(o))


def aligned(index, size):
    return pl.ds(pl.multiple_of(index * size, size), size)


def far_first(step):
    half = (step + 1) // 2
    return lax.rem(4 + half - 2 * half * lax.rem(step, 2) + 8, 8)


def mixer_kernel(
    x_ref,
    narrow_hbm,
    broad_hbm,
    w1_hbm,
    b1_hbm,
    w2_hbm,
    b2_hbm,
    landed,
    narrow,
    broad,
    w1_ref,
    b1_ref,
    w2_ref,
    b2_ref,
    t1,
    t2,
    t3,
    t4,
    swap,
    swap_back,
    mix1,
    mix2,
    line,
    spec,
    pair,
    by_place,
    column,
    mixed,
    back,
    wide,
    pair_back,
    waves,
    field,
    send_sem,
    recv_sem,
    table_sem,
):
    lat = lax.axis_index("lat")
    lon = lax.axis_index("lon")
    x_hi, y, core = lat // 16, lax.rem(lat // 2, 8), lax.rem(lat, 2)
    z, x_lo = lon // 2, lax.rem(lon, 2)
    z_hi = lon // 8
    norm = 1.0 / math.sqrt(t2.shape[0] // 2 * t4.shape[1])

    def build(n, table):
        fetches[n].wait()
        bases = (narrow if n < 2 else broad).at[n % 2]

        def group(g, _):
            c = bases[0, pl.ds(g, 1), :]
            s = bases[1, pl.ds(g, 1), :]
            if n == 1:
                for part in range(2):
                    near = pl.ds(16 * part, 16)
                    block = c * bases[2, near, :] + s * bases[3, near, :]
                    start = 512 * (g // 16) + 256 * part + 16 * lax.rem(g, 16)
                    table[pl.ds(pl.multiple_of(start, 16), 16), :] = block.astype(table.dtype)
            else:
                table[aligned(g, 32), :] = (c * bases[2] + s * bases[3]).astype(table.dtype)
            return 0

        lax.fori_loop(0, 32 if n < 2 else 16, group, 0)

    def join(w_ref, mix):
        mix[:128, :128] = w_ref[0, 0]
        mix[:128, 128:] = w_ref[1, 0]
        mix[128:, :128] = -w_ref[1, 0]
        mix[128:, 128:] = w_ref[0, 0]

    barrier = pltpu.get_barrier_semaphore()

    def greet_lon(step, _):
        peer = lax.rem(lon + step, 16)
        pl.semaphore_signal(barrier, inc=1, device_id={"lon": peer}, device_id_type=MESH)
        return 0

    def greet_lat(step, _):
        peer = lax.rem(lat + 2 * step, 32)
        pl.semaphore_signal(barrier, inc=1, device_id={"lat": peer}, device_id_type=MESH)
        return 0

    sibling = lat + 1 - 2 * core
    lax.fori_loop(1, 16, greet_lon, 0)
    lax.fori_loop(1, 16, greet_lat, 0)
    pl.semaphore_signal(barrier, inc=1, device_id={"lat": sibling}, device_id_type=MESH)
    fetches = [
        pltpu.make_async_copy(hbm.at[n], vmem.at[n], table_sem.at[2 * m + n])
        for m, (hbm, vmem) in enumerate(((narrow_hbm, narrow), (broad_hbm, broad)))
        for n in range(2)
    ] + [
        pltpu.make_async_copy(hbm, vmem, table_sem.at[4 + n])
        for n, (hbm, vmem) in enumerate(
            ((w1_hbm, w1_ref), (b1_hbm, b1_ref), (w2_hbm, w2_ref), (b2_hbm, b2_ref))
        )
    ]
    for copy in fetches:
        copy.start()

    pl.semaphore_wait(barrier, 31)

    def lon_peer(step):
        return lax.rem(z + far_first(step // 2), 8) * 2 + lax.rem(x_lo + 1 + step, 2)

    def push(slot, axis, steps, peer_of, source, target):
        def send(step, _):
            peer = peer_of(step)
            pltpu.make_async_remote_copy(
                src_ref=source(peer),
                dst_ref=target,
                send_sem=send_sem.at[slot],
                recv_sem=recv_sem.at[slot],
                device_id={axis: peer},
                device_id_type=MESH,
            ).start()
            return 0

        lax.fori_loop(steps[0], steps[1], send, 0)

    def keep(slot, source, target):
        pltpu.make_async_copy(source, target, recv_sem.at[slot]).start()

    def arrived(slot, landing):
        pltpu.make_async_copy(landing, landing, recv_sem.at[slot]).wait()

    def to_sibling(slot, source, target):
        pltpu.make_async_remote_copy(
            src_ref=source,
            dst_ref=target,
            send_sem=send_sem.at[slot],
            recv_sem=recv_sem.at[slot],
            device_id={"lat": sibling},
            device_id_type=MESH,
        ).start()

    ys = [lax.rem(y + step, 8) for step in range(8)]
    zs = [lax.rem(z + step, 8) for step in range(8)]
    his = [x_hi, 1 - x_hi]
    los = [x_lo, 1 - x_lo]
    place = ((x_hi * 8 + y) * 8 + z) * 2 + x_lo

    def to_chips(slot, source, landing):
        keep(slot, source.at[aligned(place, 4)], landing.at[aligned(place, 4)])
        for dy, dz, dh, dl in wide_order():
            other = ((his[dh] * 8 + ys[dy]) * 8 + zs[dz]) * 2 + los[dl]
            pltpu.make_async_remote_copy(
                src_ref=source.at[aligned(other, 4)],
                dst_ref=landing.at[aligned(place, 4)],
                send_sem=send_sem.at[slot],
                recv_sem=recv_sem.at[slot],
                device_id={
                    "lat": (his[dh] * 8 + ys[dy]) * 2 + core,
                    "lon": zs[dz] * 2 + los[dl],
                },
                device_id_type=MESH,
            ).start()

    keep(0, x_ref.at[lon], line.at[aligned(lon, 64)])
    push(0, "lon", (0, 15), lon_peer, lambda p: x_ref.at[p], line.at[aligned(lon, 64)])
    build(0, t1)
    row = lax.broadcasted_iota(jnp.int32, swap.shape, 0)
    col = lax.broadcasted_iota(jnp.int32, swap.shape, 1)
    source = row // 2 % 2 * 128 + row // 4 * 2 + row % 2
    swap[...] = jnp.where(col == source, 1.0, 0.0).astype(swap.dtype)
    source = col // 2 % 2 * 128 + col // 4 * 2 + col % 2
    swap_back[...] = jnp.where(row == source, 1.0, 0.0).astype(swap.dtype)
    arrived(0, line)

    def fold(block, sign):
        return (block[:512].astype(jnp.float32) + sign * block[512:].astype(jnp.float32)).astype(
            block.dtype
        )

    def half_of(parity):
        rows = pl.ds(pl.multiple_of(512 * parity, 512), 512)
        operand = fold(line[...], (1 - 2 * parity).astype(jnp.float32))
        return jnp.dot(t1[rows, :], operand, preferred_element_type=jnp.float32).astype(spec.dtype)

    spec[...] = half_of(1 - core)
    to_sibling(1, spec, pair.at[core])
    pair[core] = half_of(core)
    arrived(1, spec)

    for block in range(4):
        both = pair[:, 128 * block : 128 * block + 128, :].reshape(256, -1)
        both = jnp.dot(swap[...], both, preferred_element_type=jnp.float32)
        by_place[256 * block : 256 * block + 256, :] = both.astype(by_place.dtype)
    to_chips(2, by_place, column)
    build(1, t2)
    build(2, t3)
    for copy in fetches[4:]:
        copy.wait()
    join(w1_ref, mix1)
    join(w2_ref, mix2)
    bias1 = jnp.concatenate([b1_ref[0], b1_ref[1]], axis=1)
    bias2 = jnp.concatenate([b2_ref[0], b2_ref[1]], axis=1)
    weight = jnp.where(lat + lon == 0, 0.5, 1.0)
    arrived(2, column)

    def shrink(v):
        return jnp.maximum(v - shrink_level, 0.0) + jnp.minimum(v + shrink_level, 0.0)

    for parity in range(2):
        rows = pl.ds(512 * parity, 512)
        spectrum = jnp.dot(
            t2[rows, :], fold(column[...], 1.0 - 2.0 * parity), preferred_element_type=jnp.float32
        )
        spectrum = (spectrum * norm).astype(jnp.bfloat16)
        spectrum = jnp.concatenate([spectrum[:256], spectrum[256:]], axis=1)
        hidden = jnp.dot(spectrum, mix1[...], preferred_element_type=jnp.float32)
        hidden = jnp.maximum(hidden + bias1, 0.0).astype(jnp.bfloat16)
        result = jnp.dot(hidden, mix2[...], preferred_element_type=jnp.float32)
        result = (shrink(result + bias2) * weight).astype(jnp.bfloat16)
        mixed[512 * parity : 512 * parity + 256] = result[:, :128]
        mixed[512 * parity + 256 : 512 * parity + 512] = result[:, 128:]

    even = jnp.dot(t3[:, :512], mixed[:512], preferred_element_type=jnp.float32)
    odd = jnp.dot(t3[:, 512:], mixed[512:], preferred_element_type=jnp.float32)
    back[:512] = (even + odd).astype(back.dtype)
    back[512:] = (even - odd).astype(back.dtype)
    to_chips(3, back, wide)
    build(3, t4)
    arrived(3, wide)

    for block in range(4):
        both = wide[256 * block : 256 * block + 256, :]
        both = jnp.dot(swap_back[...], both, preferred_element_type=jnp.float32)
        both = both.astype(wide.dtype).reshape(2, 128, -1)
        pair_back[:, 128 * block : 128 * block + 128, :] = both
    to_sibling(4, pair_back.at[1 - core], waves)

    def part_of(parity, operand):
        columns = pl.ds(pl.multiple_of(512 * parity, 512), 512)
        return jnp.dot(t4[:, columns], operand, preferred_element_type=jnp.float32)

    held = part_of(core, pair_back[core])
    arrived(4, waves)
    fresh = part_of(1 - core, waves[...])
    for turn, half in enumerate((1 - z_hi, z_hi)):
        sign = (1 - 2 * half).astype(jnp.float32)
        scale = (1 - 2 * half * core).astype(jnp.float32) * (2.0 * norm)
        filtered = (held + sign * fresh) * scale
        cells = pl.ds(pl.multiple_of(512 * half, 512), 512)
        total = line[cells, :].astype(jnp.float32) + filtered.astype(field.dtype).astype(jnp.float32)
        field[512 * turn : 512 * turn + 512, :] = total.astype(field.dtype)

        def block_of(peer, turn=turn):
            return field.at[pl.ds(pl.multiple_of(512 * turn + 64 * lax.rem(peer, 8), 64), 64)]

        if turn == 1:
            keep(5, block_of(lon), landed.at[lon])
        push(
            5,
            "lon",
            (turn, 8),
            lambda step, half=half: half * 8 + lax.rem(lon + step, 8),
            block_of,
            landed.at[lon],
        )
    arrived(5, landed)

    for slot, sent in enumerate((960, 512, 1020, 1020, 512, 960)):
        left = line.at[pl.ds(0, sent)]
        pltpu.make_async_copy(left, left, send_sem.at[slot]).wait()


def body(features, w_first, bias_first, w_second, bias_second):
    lat_rows, lon_cells, channels = features.shape
    lat_count, lon_count = lax.axis_size("lat"), lax.axis_size("lon")
    total_lat, total_lon = lat_rows * lat_count, lon_cells * lon_count
    narrow, broad = (jnp.asarray(t) for t in table_bases(total_lat, total_lon))
    hbm = pl.BlockSpec(memory_space=pltpu.HBM)
    half = jnp.bfloat16
    flat = pltpu.VMEM((1024, channels), half)
    tables = [pltpu.VMEM(shape, half) for shape in [(1024, 512)] * 2 + [(512, 1024)] * 2]
    return pl.pallas_call(
        mixer_kernel,
        out_shape=jax.ShapeDtypeStruct((lat_rows, lon_cells, channels), half),
        in_specs=[hbm] * 7,
        out_specs=pl.BlockSpec(memory_space=pltpu.VMEM),
        scratch_shapes=[
            pltpu.VMEM(a.shape, a.dtype)
            for a in (narrow, broad, w_first, bias_first, w_second, bias_second)
        ]
        + tables
        + [
            pltpu.VMEM((256, 256), half),
            pltpu.VMEM((256, 256), half),
            pltpu.VMEM((256, 256), half),
            pltpu.VMEM((256, 256), half),
            flat,
            pltpu.VMEM((512, channels), half),
            pltpu.VMEM((2, 512, channels), half),
            flat,
            flat,
            flat,
            flat,
            flat,
            pltpu.VMEM((2, 512, channels), half),
            pltpu.VMEM((512, channels), half),
            flat,
            pltpu.SemaphoreType.DMA((6,)),
            pltpu.SemaphoreType.DMA((6,)),
            pltpu.SemaphoreType.DMA((8,)),
        ],
        compiler_params=pltpu.CompilerParams(
            collective_id=0, has_side_effects=True, vmem_limit_bytes=40 * 2**20
        ),
    )(
        *(
            pltpu.with_memory_space_constraint(a, pltpu.HBM)
            for a in (features, narrow, broad, w_first, bias_first, w_second, bias_second)
        )
    )


def solution(mesh):
    in_specs = (P("lat", "lon", None), P(), P(), P(), P())
    out_specs = P("lat", "lon", None)
    return jax.shard_map(
        body, mesh=mesh, in_specs=in_specs, out_specs=out_specs, check_vma=False
    )
```

```python
import functools
import math

import jax
import jax.numpy as jnp
import numpy as np
from jax import lax
from jax.experimental import pallas as pl
from jax.experimental.pallas import tpu as pltpu
from jax.sharding import PartitionSpec as P

shrink_level = 0.01
MESH = pl.DeviceIdType.MESH


def wave(turn, length):
    angle = (turn % length) * (2.0 * math.pi / length)
    return np.cos(angle), np.sin(angle)


def table_bases(total_lat, total_lon):
    cells = np.arange(total_lon // 2)
    fine = np.arange(16)
    place, core = np.arange(total_lat // 2) // 2, np.arange(total_lat // 2) % 2
    row = 16 * (place // 16 * 2 + core) + place % 16
    lon_waves = np.arange(total_lon // 2).reshape(-1, 2).T.reshape(-1)
    lat_waves = np.arange(total_lat).reshape(-1, 2).T.reshape(2, -1)
    c, s = wave(np.outer(lon_waves[::16], cells), total_lon)
    pc, ps = wave(2 * np.outer(fine, cells), total_lon)
    p = np.stack([pc, -ps], axis=1).reshape(32, -1)
    q = np.stack([-ps, -pc], axis=1).reshape(32, -1)
    narrow = [(c, s, p, q)]
    c, s = wave(np.outer(lat_waves.reshape(-1)[::16], np.repeat(row, 2)), total_lat)
    pc, ps = wave(2 * np.outer(fine, row), total_lat)
    p = np.stack([np.stack([pc, ps], 2), np.stack([-ps, pc], 2)]).reshape(32, -1)
    q = np.stack([np.stack([-ps, pc], 2), np.stack([-pc, -ps], 2)]).reshape(32, -1)
    narrow.append((c, s, p, q))
    columns = np.stack([lat_waves, lat_waves], axis=1).reshape(-1)
    c, s = wave(np.outer(np.tile(row[::16], 2), columns), total_lat)
    pc, ps = wave(np.outer(row[:16], lat_waves), total_lat)
    pc, ps = pc.reshape(16, 2, -1), ps.reshape(16, 2, -1)
    p = np.stack([np.stack([pc, -ps], 2), np.stack([ps, pc], 2)], 1).reshape(32, -1)
    q = np.stack([np.stack([-ps, -pc], 2), np.stack([pc, -ps], 2)], 1).reshape(32, -1)
    broad = [(c, s, p, q)]
    c, s = wave(np.outer(np.tile(cells[::32], 2), np.repeat(lon_waves, 2)), total_lon)
    pc, ps = wave(np.outer(np.arange(32), lon_waves), total_lon)
    p = np.stack([pc, -ps], axis=2).reshape(32, -1)
    q = np.stack([-ps, -pc], axis=2).reshape(32, -1)
    broad.append((c, s, p, q))
    return [np.array(t).astype(np.float32) for t in (narrow, broad)]


def wide_order():
    def hops(o):
        return min(o[0], 8 - o[0]) + min(o[1], 8 - o[1]) + 2 * o[2] + o[3]

    offsets = [(y, z, h, l) for y in range(8) for z in range(8) for h in range(2) for l in range(2)]
    return sorted(offsets[1:], key=lambda o: -hops(o))


def aligned(index, size):
    return pl.ds(pl.multiple_of(index * size, size), size)


def far_first(step):
    half = (step + 1) // 2
    return lax.rem(4 + half - 2 * half * lax.rem(step, 2) + 8, 8)


def mixer_kernel(
    x_ref,
    narrow_hbm,
    broad_hbm,
    w1_hbm,
    b1_hbm,
    w2_hbm,
    b2_hbm,
    landed,
    narrow,
    broad,
    w1_ref,
    b1_ref,
    w2_ref,
    b2_ref,
    t1,
    t2,
    t3,
    t4,
    swap,
    swap_back,
    mix1,
    mix2,
    line,
    spec,
    pair,
    by_place,
    column,
    mixed,
    back,
    wide,
    pair_back,
    waves,
    field,
    send_sem,
    recv_sem,
    table_sem,
):
    lat = lax.axis_index("lat")
    lon = lax.axis_index("lon")
    x_hi, y, core = lat // 16, lax.rem(lat // 2, 8), lax.rem(lat, 2)
    z, x_lo = lon // 2, lax.rem(lon, 2)
    z_hi = lon // 8
    norm = 1.0 / math.sqrt(t2.shape[0] // 2 * t4.shape[1])

    def build(n, table):
        fetches[n].wait()
        bases = (narrow if n < 2 else broad).at[n % 2]

        def group(g, _):
            c = bases[0, pl.ds(g, 1), :]
            s = bases[1, pl.ds(g, 1), :]
            if n == 1:
                for part in range(2):
                    near = pl.ds(16 * part, 16)
                    block = c * bases[2, near, :] + s * bases[3, near, :]
                    start = 512 * (g // 16) + 256 * part + 16 * lax.rem(g, 16)
                    table[pl.ds(pl.multiple_of(start, 16), 16), :] = block.astype(table.dtype)
            else:
                table[aligned(g, 32), :] = (c * bases[2] + s * bases[3]).astype(table.dtype)
            return 0

        lax.fori_loop(0, 32 if n < 2 else 16, group, 0)

    def join(w_ref, mix):
        mix[:128, :128] = w_ref[0, 0]
        mix[:128, 128:] = w_ref[1, 0]
        mix[128:, :128] = -w_ref[1, 0]
        mix[128:, 128:] = w_ref[0, 0]

    barrier = pltpu.get_barrier_semaphore()

    def greet_lon(step, _):
        peer = lax.rem(lon + step, 16)
        pl.semaphore_signal(barrier, inc=1, device_id={"lon": peer}, device_id_type=MESH)
        return 0

    def greet_lat(step, _):
        peer = lax.rem(lat + 2 * step, 32)
        pl.semaphore_signal(barrier, inc=1, device_id={"lat": peer}, device_id_type=MESH)
        return 0

    sibling = lat + 1 - 2 * core
    lax.fori_loop(1, 16, greet_lon, 0)
    lax.fori_loop(1, 16, greet_lat, 0)
    pl.semaphore_signal(barrier, inc=1, device_id={"lat": sibling}, device_id_type=MESH)
    pl.semaphore_wait(barrier, 31)

    def lon_peer(step):
        return lax.rem(z + far_first(step // 2), 8) * 2 + lax.rem(x_lo + 1 + step, 2)

    def push(slot, axis, steps, peer_of, source, target):
        def send(step, _):
            peer = peer_of(step)
            pltpu.make_async_remote_copy(
                src_ref=source(peer),
                dst_ref=target,
                send_sem=send_sem.at[slot],
                recv_sem=recv_sem.at[slot],
                device_id={axis: peer},
                device_id_type=MESH,
            ).start()
            return 0

        lax.fori_loop(steps[0], steps[1], send, 0)

    def keep(slot, source, target):
        pltpu.make_async_copy(source, target, recv_sem.at[slot]).start()

    def arrived(slot, landing):
        pltpu.make_async_copy(landing, landing, recv_sem.at[slot]).wait()

    def to_sibling(slot, source, target):
        pltpu.make_async_remote_copy(
            src_ref=source,
            dst_ref=target,
            send_sem=send_sem.at[slot],
            recv_sem=recv_sem.at[slot],
            device_id={"lat": sibling},
            device_id_type=MESH,
        ).start()

    ys = [lax.rem(y + step, 8) for step in range(8)]
    zs = [lax.rem(z + step, 8) for step in range(8)]
    his = [x_hi, 1 - x_hi]
    los = [x_lo, 1 - x_lo]
    place = ((x_hi * 8 + y) * 8 + z) * 2 + x_lo

    def to_chips(slot, source, landing):
        keep(slot, source.at[aligned(place, 4)], landing.at[aligned(place, 4)])
        for dy, dz, dh, dl in wide_order():
            other = ((his[dh] * 8 + ys[dy]) * 8 + zs[dz]) * 2 + los[dl]
            pltpu.make_async_remote_copy(
                src_ref=source.at[aligned(other, 4)],
                dst_ref=landing.at[aligned(place, 4)],
                send_sem=send_sem.at[slot],
                recv_sem=recv_sem.at[slot],
                device_id={
                    "lat": (his[dh] * 8 + ys[dy]) * 2 + core,
                    "lon": zs[dz] * 2 + los[dl],
                },
                device_id_type=MESH,
            ).start()

    keep(0, x_ref.at[lon], line.at[aligned(lon, 64)])
    push(0, "lon", (0, 15), lon_peer, lambda p: x_ref.at[p], line.at[aligned(lon, 64)])
    fetches = [
        pltpu.make_async_copy(hbm.at[n], vmem.at[n], table_sem.at[2 * m + n])
        for m, (hbm, vmem) in enumerate(((narrow_hbm, narrow), (broad_hbm, broad)))
        for n in range(2)
    ] + [
        pltpu.make_async_copy(hbm, vmem, table_sem.at[4 + n])
        for n, (hbm, vmem) in enumerate(
            ((w1_hbm, w1_ref), (b1_hbm, b1_ref), (w2_hbm, w2_ref), (b2_hbm, b2_ref))
        )
    ]
    for copy in fetches:
        copy.start()

    build(0, t1)
    row = lax.broadcasted_iota(jnp.int32, swap.shape, 0)
    col = lax.broadcasted_iota(jnp.int32, swap.shape, 1)
    source = row // 2 % 2 * 128 + row // 4 * 2 + row % 2
    swap[...] = jnp.where(col == source, 1.0, 0.0).astype(swap.dtype)
    source = col // 2 % 2 * 128 + col // 4 * 2 + col % 2
    swap_back[...] = jnp.where(row == source, 1.0, 0.0).astype(swap.dtype)
    arrived(0, line)

    def fold(block, sign):
        return (block[:512].astype(jnp.float32) + sign * block[512:].astype(jnp.float32)).astype(
            block.dtype
        )

    def half_of(parity):
        rows = pl.ds(pl.multiple_of(512 * parity, 512), 512)
        operand = fold(line[...], (1 - 2 * parity).astype(jnp.float32))
        return jnp.dot(t1[rows, :], operand, preferred_element_type=jnp.float32).astype(spec.dtype)

    spec[...] = half_of(1 - core)
    to_sibling(1, spec, pair.at[core])
    pair[core] = half_of(core)
    arrived(1, spec)

    for block in range(4):
        both = pair[:, 128 * block : 128 * block + 128, :].reshape(256, -1)
        both = jnp.dot(swap[...], both, preferred_element_type=jnp.float32)
        by_place[256 * block : 256 * block + 256, :] = both.astype(by_place.dtype)
    to_chips(2, by_place, column)
    build(1, t2)
    build(2, t3)
    for copy in fetches[4:]:
        copy.wait()
    join(w1_ref, mix1)
    join(w2_ref, mix2)
    bias1 = jnp.concatenate([b1_ref[0], b1_ref[1]], axis=1)
    bias2 = jnp.concatenate([b2_ref[0], b2_ref[1]], axis=1)
    weight = jnp.where(lat + lon == 0, 0.5, 1.0)
    arrived(2, column)

    def shrink(v):
        return jnp.maximum(v - shrink_level, 0.0) + jnp.minimum(v + shrink_level, 0.0)

    for parity in range(2):
        rows = pl.ds(512 * parity, 512)
        spectrum = jnp.dot(
            t2[rows, :], fold(column[...], 1.0 - 2.0 * parity), preferred_element_type=jnp.float32
        )
        spectrum = (spectrum * norm).astype(jnp.bfloat16)
        spectrum = jnp.concatenate([spectrum[:256], spectrum[256:]], axis=1)
        hidden = jnp.dot(spectrum, mix1[...], preferred_element_type=jnp.float32)
        hidden = jnp.maximum(hidden + bias1, 0.0).astype(jnp.bfloat16)
        result = jnp.dot(hidden, mix2[...], preferred_element_type=jnp.float32)
        result = (shrink(result + bias2) * weight).astype(jnp.bfloat16)
        mixed[512 * parity : 512 * parity + 256] = result[:, :128]
        mixed[512 * parity + 256 : 512 * parity + 512] = result[:, 128:]

    even = jnp.dot(t3[:, :512], mixed[:512], preferred_element_type=jnp.float32)
    odd = jnp.dot(t3[:, 512:], mixed[512:], preferred_element_type=jnp.float32)
    back[:512] = (even + odd).astype(back.dtype)
    back[512:] = (even - odd).astype(back.dtype)
    to_chips(3, back, wide)
    build(3, t4)
    arrived(3, wide)

    for block in range(4):
        both = wide[256 * block : 256 * block + 256, :]
        both = jnp.dot(swap_back[...], both, preferred_element_type=jnp.float32)
        both = both.astype(wide.dtype).reshape(2, 128, -1)
        pair_back[:, 128 * block : 128 * block + 128, :] = both
    to_sibling(4, pair_back.at[1 - core], waves)

    def part_of(parity, operand):
        columns = pl.ds(pl.multiple_of(512 * parity, 512), 512)
        return jnp.dot(t4[:, columns], operand, preferred_element_type=jnp.float32)

    held = part_of(core, pair_back[core])
    arrived(4, waves)
    fresh = part_of(1 - core, waves[...])
    for turn, half in enumerate((1 - z_hi, z_hi)):
        sign = (1 - 2 * half).astype(jnp.float32)
        scale = (1 - 2 * half * core).astype(jnp.float32) * (2.0 * norm)
        filtered = (held + sign * fresh) * scale
        cells = pl.ds(pl.multiple_of(512 * half, 512), 512)
        total = line[cells, :].astype(jnp.float32) + filtered.astype(field.dtype).astype(jnp.float32)
        field[512 * turn : 512 * turn + 512, :] = total.astype(field.dtype)

        def block_of(peer, turn=turn):
            return field.at[pl.ds(pl.multiple_of(512 * turn + 64 * lax.rem(peer, 8), 64), 64)]

        if turn == 1:
            keep(5, block_of(lon), landed.at[lon])
        push(
            5,
            "lon",
            (turn, 8),
            lambda step, half=half: half * 8 + lax.rem(lon + step, 8),
            block_of,
            landed.at[lon],
        )
    arrived(5, landed)

    for slot, sent in enumerate((960, 512, 1020, 1020, 512, 960)):
        left = line.at[pl.ds(0, sent)]
        pltpu.make_async_copy(left, left, send_sem.at[slot]).wait()


def body(features, w_first, bias_first, w_second, bias_second):
    lat_rows, lon_cells, channels = features.shape
    lat_count, lon_count = lax.axis_size("lat"), lax.axis_size("lon")
    total_lat, total_lon = lat_rows * lat_count, lon_cells * lon_count
    narrow, broad = (jnp.asarray(t) for t in table_bases(total_lat, total_lon))
    hbm = pl.BlockSpec(memory_space=pltpu.HBM)
    half = jnp.bfloat16
    flat = pltpu.VMEM((1024, channels), half)
    tables = [pltpu.VMEM(shape, half) for shape in [(1024, 512)] * 2 + [(512, 1024)] * 2]
    return pl.pallas_call(
        mixer_kernel,
        out_shape=jax.ShapeDtypeStruct((lat_rows, lon_cells, channels), half),
        in_specs=[hbm] * 7,
        out_specs=pl.BlockSpec(memory_space=pltpu.VMEM),
        scratch_shapes=[
            pltpu.VMEM(a.shape, a.dtype)
            for a in (narrow, broad, w_first, bias_first, w_second, bias_second)
        ]
        + tables
        + [
            pltpu.VMEM((256, 256), half),
            pltpu.VMEM((256, 256), half),
            pltpu.VMEM((256, 256), half),
            pltpu.VMEM((256, 256), half),
            flat,
            pltpu.VMEM((512, channels), half),
            pltpu.VMEM((2, 512, channels), half),
            flat,
            flat,
            flat,
            flat,
            flat,
            pltpu.VMEM((2, 512, channels), half),
            pltpu.VMEM((512, channels), half),
            flat,
            pltpu.SemaphoreType.DMA((6,)),
            pltpu.SemaphoreType.DMA((6,)),
            pltpu.SemaphoreType.DMA((8,)),
        ],
        compiler_params=pltpu.CompilerParams(
            collective_id=0, has_side_effects=True, vmem_limit_bytes=40 * 2**20
        ),
    )(
        *(
            pltpu.with_memory_space_constraint(a, pltpu.HBM)
            for a in (features, narrow, broad, w_first, bias_first, w_second, bias_second)
        )
    )


def solution(mesh):
    in_specs = (P("lat", "lon", None), P(), P(), P(), P())
    out_specs = P("lat", "lon", None)
    return jax.shard_map(
        body, mesh=mesh, in_specs=in_specs, out_specs=out_specs, check_vma=False
    )
```
